32 devices in a mesh: tm: 4 (over y, x), space: 8 (over z, core).
Axes of the slice: x: 2, y: 2, z: 4, core: 2. Of those that a mesh axis runs over, the one named last changes fastest.
Arguments:
- vectors: float32 [4, 2, 3, 64, 2048], P('tm', None, None, None, 'space'), may hold values from -6 to 6
- perambulators: float32 [4, 16, 2, 4096], P('tm'), may hold values from -0.75 to 0.75
- shift_steps: int32 [4], P('tm'), may hold values from 1 to 3, as said below
- spin_choice: int32 [4, 3], replicated, may hold values from 0 to 15
Outputs:
- elementals: float32 [4, 64, 2, 4096], P('tm', 'space')
- correlator: float32 [4, 4, 2], P('tm')
The draws below stay inside these ranges and needn't reach their ends.
Inputs may be any that keep to these rules, and one draw needn't show every extreme that they name: `shift_steps`: every distance from 1 to 3 is taken by at least one source timeslice. `spin_choice`: each entry is alpha 4 + beta for a pair of spin indices.
All inputs are finite; a program needn't handle non-finite values.
Results may differ from the reference program's by a relative error of at most 0.0003.
Values sent between devices are 32-bit elements; how exact they have to be, the bound alone decides.
A program may use at most 64 MiB of HBM per device.

```python
import math
import jax
import jax.numpy as jnp
from jax import lax

NVEC = 64
SPIN = 4
COMBOS = 4
NSITES = 2048
NT = 4


def draw_shift_steps(key, part):
    every_step = jnp.arange(1, NT, dtype=jnp.int32)
    extra_step = jax.random.randint(jax.random.fold_in(key, 17), (1,), 1, NT, dtype=jnp.int32)
    pooled = jnp.concatenate([every_step, extra_step], axis=0)
    return jax.random.permutation(jax.random.fold_in(key, 29), pooled).astype(jnp.int32)


def with_ends(entries, stream_key, smallest, top_value):
    index_at = [jax.random.randint(jax.random.fold_in(stream_key, axis), (), 0, length) for axis, length in enumerate(entries.shape)]
    longest = entries.shape.index(max(entries.shape))
    beside = index_at[:longest] + [(index_at[longest] + 1) % entries.shape[longest]] + index_at[longest + 1:]
    return entries.at[tuple(index_at)].set(smallest).at[tuple(beside)].set(top_value)


def shard_levels(own_key, dims, pieces, low, largest):
    factor_of = 1.0
    for axis_at, blocks in pieces:
        heights = jax.random.uniform(jax.random.fold_in(jax.random.fold_in(own_key, 6), axis_at), (blocks,), jnp.float32, low / len(pieces), largest / len(pieces))
        factor_of = factor_of * jnp.repeat(jnp.exp(heights), dims[axis_at] // blocks).reshape((-1,) + (1,) * (len(dims) - 1 - axis_at))
    return factor_of


def gaussian(stream_key, shape, spread, limit, pieces=(), kind=jnp.bfloat16):
    array = spread * jax.random.normal(stream_key, shape, jnp.float32)
    if pieces:
        array = array * shard_levels(stream_key, shape, pieces, -0.22, 0.18)
    return jnp.clip(array, -limit, limit).astype(kind)


def setup_inputs(seed: int = 0) -> dict:
    streams_of = jax.random.split(jax.random.key(seed), 5)
    return {
        "vectors": gaussian(streams_of[0], (NT, 2, 3, NVEC, NSITES), 1.0, 6.0, ((0, 4), (4, 8)), jnp.float32),
        "perambulators": gaussian(streams_of[1], (NT, SPIN * SPIN, 2, NVEC * NVEC), NVEC ** -0.5, 0.75, ((0, 4),), jnp.float32),
        "shift_steps": draw_shift_steps(jax.random.fold_in(streams_of[4], 71), 0),
        "spin_choice": with_ends(jax.random.randint(streams_of[3], (COMBOS, 3), 0, SPIN * SPIN), jax.random.fold_in(streams_of[3], 1), 0, (SPIN * SPIN) - 1).astype(jnp.int32),
    }


exact_mode = lax.Precision.HIGHEST

def complex_product(left_re, left_im, right_re, right_im):
    return (left_re * right_re - left_im * right_im, left_re * right_im + left_im * right_re)

def rotate(values, places):
    return jnp.concatenate([values[places:], values[:places]], axis=0)

def contract_first(left, right):
    return lax.dot_general(left, right, (((0,), (0,)), ((), ())), precision=exact_mode)

def inner_rows(left, right):
    return lax.dot_general(left, right, (((1,), (1,)), ((), ())), precision=exact_mode)

def complex_einsum(form, left, right):
    first = jnp.einsum(form, left[0], right[0], precision=exact_mode) - jnp.einsum(form, left[1], right[1], precision=exact_mode)
    second = jnp.einsum(form, left[0], right[1], precision=exact_mode) + jnp.einsum(form, left[1], right[0], precision=exact_mode)
    return (first, second)

def elemental_rows(vec_re, vec_im, lead_re, lead_im, first_row, row_count, factor):
    sites = vec_re.shape[1]
    nvec = vec_re.shape[2]
    block = math.gcd(row_count, 4)

    def one_block(index):
        offset = (first_row + index * block).astype(jnp.int32)
        part_re = lax.dynamic_slice_in_dim(vec_re, offset, block, 2)[:, :, :, None]
        part_im = lax.dynamic_slice_in_dim(vec_im, offset, block, 2)[:, :, :, None]
        full_re = vec_re[:, :, None, :]
        full_im = vec_im[:, :, None, :]
        one_re, one_im = complex_product(rotate(part_re, 1), rotate(part_im, 1), rotate(full_re, 2), rotate(full_im, 2))
        two_re, two_im = complex_product(rotate(part_re, 2), rotate(part_im, 2), rotate(full_re, 1), rotate(full_im, 1))
        cross_re = (one_re - two_re).reshape(3 * sites, block * nvec)
        cross_im = (one_im - two_im).reshape(3 * sites, block * nvec)
        out_re = contract_first(lead_re, cross_re) - contract_first(lead_im, cross_im)
        out_im = contract_first(lead_re, cross_im) + contract_first(lead_im, cross_re)
        stacked = jnp.stack([out_re, out_im], 0).reshape(2, nvec, block, nvec)
        return jnp.transpose(stacked, (2, 0, 1, 3)).reshape(block, 2, nvec * nvec) * factor
    result = lax.map(one_block, jnp.arange(row_count // block, dtype=jnp.int32))
    return result.reshape(row_count, 2, nvec * nvec)

def transform_rows(own, mats, nvec):
    combos = mats.shape[0]
    row_count = own.shape[0]
    elem = (own[:, 0].reshape(row_count, nvec, nvec), own[:, 1].reshape(row_count, nvec, nvec))
    first_mat = (mats[:, 0, 0].reshape(combos, nvec, nvec), mats[:, 0, 1].reshape(combos, nvec, nvec))
    third_mat = (mats[:, 2, 0].reshape(combos, nvec, nvec), mats[:, 2, 1].reshape(combos, nvec, nvec))
    half = complex_einsum('jik,slk->sjil', elem, third_mat)
    done = complex_einsum('smi,sjil->sjml', first_mat, half)
    return (done[0].reshape(combos * row_count, nvec * nvec), done[1].reshape(combos * row_count, nvec * nvec))

def pair_sum(sink_rows, trans_re, trans_im, mid_re, mid_im):
    combos = mid_re.shape[0]
    sink_count = sink_rows.shape[0]
    own_count = mid_re.shape[2]
    sink_re = sink_rows[:, 0]
    sink_im = sink_rows[:, 1]
    inner_re = (inner_rows(sink_re, trans_re) + inner_rows(sink_im, trans_im)).reshape(sink_count, combos, own_count)
    inner_im = (inner_rows(sink_re, trans_im) - inner_rows(sink_im, trans_re)).reshape(sink_count, combos, own_count)
    total_re = jnp.einsum('srj,rsj->s', mid_re, inner_re, precision=exact_mode) - jnp.einsum('srj,rsj->s', mid_im, inner_im, precision=exact_mode)
    total_im = jnp.einsum('srj,rsj->s', mid_re, inner_im, precision=exact_mode) + jnp.einsum('srj,rsj->s', mid_im, inner_re, precision=exact_mode)
    return jnp.stack([total_re, total_im], -1)

def reference(vectors, perambulators, shift_steps, spin_choice):
    factor = 1.0 / math.sqrt(24.0 * NSITES)
    corr_factor = 0.25 / (NVEC * math.sqrt(NVEC))

    def one_time(vec):
        vec_re = jnp.transpose(vec[0], (0, 2, 1))
        vec_im = jnp.transpose(vec[1], (0, 2, 1))
        lead_re = vec_re.reshape(3 * NSITES, NVEC)
        lead_im = vec_im.reshape(3 * NSITES, NVEC)
        return elemental_rows(vec_re, vec_im, lead_re, lead_im, 0, NVEC, factor)
    elementals = lax.map(one_time, vectors)
    targets = ((jnp.arange(NT, dtype=jnp.int32) + shift_steps.astype(jnp.int32)) % NT).astype(jnp.int32)
    sinks = jnp.take(elementals, targets, axis=0)

    def one_pair(packed):
        own, sink, peram = packed
        mats = peram[spin_choice]
        trans_re, trans_im = transform_rows(own, mats, NVEC)
        mid_re = mats[:, 1, 0].reshape(COMBOS, NVEC, NVEC)
        mid_im = mats[:, 1, 1].reshape(COMBOS, NVEC, NVEC)
        return pair_sum(sink, trans_re, trans_im, mid_re, mid_im) * corr_factor
    correlator = lax.map(one_pair, (elementals, sinks, perambulators))
    return (elementals, correlator)
```

```python
import functools
import math

import jax
import jax.numpy as jnp
from jax import lax
from jax.experimental import pallas as pl
from jax.experimental.pallas import tpu as pltpu
from jax.sharding import PartitionSpec as P

MESH = pl.DeviceIdType.MESH
VM = pl.BlockSpec(memory_space=pltpu.VMEM)
NT_DIMS = (((1,), (1,)), ((), ()))


def halves(x):
    top = x.astype(jnp.bfloat16)
    return top, (x - top.astype(jnp.float32)).astype(jnp.bfloat16)


def dot(a, b):
    return jnp.dot(a, b, preferred_element_type=jnp.float32)


def elementals_kernel(
    n, times, scale, corr_scale, v_ref, mats_ref, shift_ref, spin_ref, out_ref, corr_ref,
    vv, lead, d_hi, d_lo, keep, give, pair_in, chip_in, own_ref, full, sink_ref,
    board, spin_mats, local_mats, right_hh, right_lo, left_hl, placed, dense_hl,
    half_hi, half_lo, cross_w, same_w, lc_hi, lc_lo, mid_ref, slabs, sl_hi, sl_lo,
    turn, pick, tile_ref, box,
    pair_send, pair_recv, chip_send, chip_recv,
    own_send, own_recv, fwd_send, fwd_recv, tm_send, tm_recv,
    sum_send, sum_recv,
):
    f32 = jnp.float32
    me = lax.axis_index("space")
    tm = lax.axis_index("tm")
    chips = n // 2
    chip = me // 2
    core = me % 2
    mate = chip * 2 + 1 - core
    nvec = v_ref.shape[2]
    sites = v_ref.shape[3]
    own = nvec // n
    half = nvec // 2
    lanes = 2 * nvec
    reach = half // 2
    share = own * reach
    per_half = n // 2
    wide = half + reach
    block_rows = wide * reach
    side = me // per_half
    other_side = 1 - side
    first = (me % per_half) * own
    combos = spin_ref.shape[0]
    count = combos * 3 * own
    low = -(-count // 16) * 16

    barrier = pltpu.get_barrier_semaphore()
    for r in range(1, n):
        pl.semaphore_signal(barrier, inc=1, device_id=(tm, (me + r) % n), device_id_type=MESH)
    for r in range(1, times):
        pl.semaphore_signal(
            barrier, inc=1, device_id=((tm + r) % times, me), device_id_type=MESH
        )

    for a in range(3):
        re = v_ref[0, a]
        im = v_ref[1, a]
        re_hi, re_lo = halves(re)
        im_hi, im_lo = halves(im)
        one = pl.ds(a * sites, sites)
        two = pl.ds((3 + a) * sites, sites)
        lead[0:nvec, one] = re_hi
        lead[0:nvec, two] = -im_hi
        lead[nvec:lanes, one] = im_hi
        lead[nvec:lanes, two] = re_hi
        lead[lanes:lanes + nvec, one] = re_lo
        lead[lanes:lanes + nvec, two] = -im_lo
        lead[lanes + nvec:2 * lanes, one] = im_lo
        lead[lanes + nvec:2 * lanes, two] = re_lo
        for c, value in enumerate((re, im)):
            for hf in range(2):
                part = value[hf * half:(hf + 1) * half]
                vv[c, a, hf * wide:hf * wide + half, :] = part
                vv[c, a, hf * wide + half:(hf + 1) * wide, :] = part[:reach]

    def window(c, x, start):
        return vv.at[c, x, pl.ds(start, own + reach), :]

    def fill(dest, slot):
        base = (dest // per_half) * wide + (dest % per_half) * own

        def step(a):
            if own % 8 == 0:
                start = pl.multiple_of(base, 8)
                mine = [[window(c, x, start)[a:a + 1, :] for x in range(3)] for c in range(2)]
                other = [
                    [window(c, x, start)[a + 1:a + 1 + reach, :] for x in range(3)] for c in range(2)
                ]
            else:
                mine = [[vv[c, x, pl.ds(base + a, 1), :] for x in range(3)] for c in range(2)]
                other = [
                    [
                        jnp.concatenate(
                            [vv[c, x, pl.ds(base + a + 1 + r, 1), :] for r in range(reach)], axis=0
                        )
                        for x in range(3)
                    ]
                    for c in range(2)
                ]
            at = pl.ds(pl.multiple_of(slot * share + a * reach, reach), reach)
            for m in range(3):
                b, d = (m + 1) % 3, (m + 2) % 3
                real_part = (
                    mine[0][b] * other[0][d] - mine[1][b] * other[1][d]
                    - (mine[0][d] * other[0][b] - mine[1][d] * other[1][b])
                )
                imag_part = (
                    mine[0][b] * other[1][d] + mine[1][b] * other[0][d]
                    - (mine[0][d] * other[1][b] + mine[1][d] * other[0][b])
                )
                for q, value in ((m, real_part), (3 + m, imag_part)):
                    hi, lo = halves(value)
                    d_hi[at, q * sites:(q + 1) * sites] = hi
                    d_lo[at, q * sites:(q + 1) * sites] = lo

        for a in range(own):
            step(a)

    def pair_copy(s):
        return pltpu.make_async_remote_copy(
            give.at[s], pair_in.at[s], pair_send.at[s], pair_recv.at[s],
            device_id=(tm, mate), device_id_type=MESH,
        )

    def chip_copy(s):
        return pltpu.make_async_remote_copy(
            keep.at[s], chip_in.at[s], chip_send.at[s], chip_recv.at[s],
            device_id=(tm, (chip + 1 + s) % chips * 2 + core), device_id_type=MESH,
        )

    def blocks(s):
        target = (chip + 1 + s) % chips * 2
        fill(target + 1 - core, 0)
        fill(target + core, 1)
        both = lax.dot_general(d_hi[...], lead[...], NT_DIMS, preferred_element_type=f32)
        rest = lax.dot_general(d_lo[...], lead[0:lanes], NT_DIMS, preferred_element_type=f32)
        got = both[:, :lanes] + (both[:, lanes:] + rest)
        give[s] = got[:share]
        keep[s] = got[share:]

    def one_chip(s, carry):
        blocks(s)
        pair_copy(s).start()
        pair_copy(s - 1).wait_recv()
        keep[s - 1] = keep[s - 1] + pair_in[s - 1]
        chip_copy(s - 1).start()
        return carry

    blocks(0)
    pl.semaphore_wait(barrier, n - 1 + times - 1)
    pair_copy(0).start()
    lax.fori_loop(1, chips, one_chip, 0)

    lane = lax.broadcasted_iota(jnp.int32, (half, lanes), 1)
    spot = lane % nvec
    left = spot < half
    real = lane < nvec
    minus_plus = jnp.where(lax.broadcasted_iota(jnp.int32, (nvec, lanes), 1) < nvec, -1.0, 1.0)

    def weave(ref):
        even = ref[pl.ds(0, half, stride=2), :]
        odd = ref[pl.ds(1, half, stride=2), :]
        return (
            jnp.where(real, even, pltpu.roll(odd, nvec, 1)),
            jnp.where(real, pltpu.roll(even, nvec, 1), odd),
        )

    for s in range(combos):
        for q in range(3):
            board[...] = mats_ref[spin_ref[s, q]]
            even, odd = weave(board)
            spin_mats[s, q, pl.ds(0, half, stride=2), :] = even
            spin_mats[s, q, pl.ds(1, half, stride=2), :] = odd
            near = spin_mats[s, q, pl.ds(pl.multiple_of(side * half, half), half), :]
            far = spin_mats[s, q, pl.ds(pl.multiple_of(other_side * half, half), half), :]
            local = jnp.concatenate([near, far], axis=0)
            local_mats[s, q] = local
            at = (s * 3 + q) * lanes
            top_hi, top_lo = halves(local)
            low_hi, low_lo = halves(minus_plus * pltpu.roll(local, nvec, 1))
            right_hh[0:nvec, at:at + lanes] = top_hi
            right_hh[nvec:lanes, at:at + lanes] = low_hi
            right_hh[lanes:lanes + nvec, at:at + lanes] = top_hi
            right_hh[lanes + nvec:2 * lanes, at:at + lanes] = low_hi
            right_lo[0:nvec, at:at + lanes] = top_lo
            right_lo[nvec:lanes, at:at + lanes] = low_lo
    pairs = ((1, 2), (0, 2), (0, 1))
    for s in range(combos):
        for p in range(3):
            q, r = pairs[p]
            both = jnp.transpose(jnp.concatenate([local_mats[s, q], local_mats[s, r]], axis=0))
            hi, lo = halves(both)
            left_hl[s * 3 + p, :, 0:lanes] = hi
            left_hl[s * 3 + p, :, lanes:2 * lanes] = lo
    for s in range(combos):
        for p in range(3):
            if own % 8 == 0:
                rows = spin_mats[s, p, pl.ds(pl.multiple_of(me * own, own), own), :]
                mid_ref[(s * 3 + p) * own:(s * 3 + p + 1) * own, :] = rows
            else:
                for r in range(own):
                    at = (s * 3 + p) * own + r
                    mid_ref[at:at + 1, :] = spin_mats[s, p, pl.ds(me * own + r, 1), :]

    last = chips - 1
    pair_copy(last).wait_recv()
    total = keep[last] + pair_in[last]
    for s in range(last):
        chip_copy(s).wait_recv()
        total = total + chip_in[s]
    own_ref[...] = total * scale

    def rows_of(d):
        start = (d // per_half) * block_rows + reach * reach + (d % per_half) * share
        return pl.ds(pl.multiple_of(start, reach), share)

    def tm_copy(r):
        return pltpu.make_async_remote_copy(
            own_ref, sink_ref.at[r - 1], tm_send.at[r - 1], tm_recv.at[r - 1],
            device_id=((tm + r) % times, me), device_id_type=MESH,
        )

    def own_copy(r):
        target = mate if r == 0 else (chip + r) % chips * 2 + core
        return pltpu.make_async_remote_copy(
            own_ref, full.at[rows_of(me)], own_send.at[r], own_recv.at[r],
            device_id=(tm, target), device_id_type=MESH,
        )

    def forward(r):
        at = rows_of((chip + chips - r) % chips * 2 + core)
        return pltpu.make_async_remote_copy(
            full.at[at], full.at[at], fwd_send.at[r - 1], fwd_recv.at[r - 1],
            device_id=(tm, mate), device_id_type=MESH,
        )

    for r in range(1, times):
        tm_copy(r).start()
    for r in range(1, chips):
        own_copy(r).start()
    own_copy(0).start()
    full[rows_of(me), :] = own_ref[...]

    for r in range(1, times):
        tm_copy(r).wait_recv()
    chosen = sink_ref[jnp.clip(times - 1 - shift_ref[0], 0, times - 2)]
    wide_lane = lax.broadcasted_iota(jnp.int32, (share, lanes), 1)
    wide_left = wide_lane % nvec < half
    swapped = jnp.where(wide_left, pltpu.roll(chosen, lanes - half, 1), pltpu.roll(chosen, half, 1))
    chosen = jnp.where(side == 1, swapped, chosen)
    step_of = lax.broadcasted_iota(jnp.int32, (share, lanes), 0) % reach
    factor = jnp.where(wide_left, 1.0 / 3.0, 1.0) * jnp.where(step_of == reach - 1, 0.5, 1.0)
    chosen = chosen * jnp.where(wide_lane < nvec, factor, -factor)
    placed[...] = jnp.zeros_like(placed)
    for a in range(own):
        if own % 8 == 0:
            start = pl.multiple_of(a * wide + first, 8)
            view = placed.at[pl.ds(start, own + reach), :]
            view[a + 1:a + 1 + reach, :] = chosen[a * reach:(a + 1) * reach]
        else:
            for r in range(reach):
                at = a * wide + first + a + 1 + r
                placed[pl.ds(at, 1), :] = chosen[a * reach + r:a * reach + r + 1]
    around = [
        placed[a * wide:a * wide + half, :] + jnp.concatenate(
            [placed[a * wide + half:(a + 1) * wide, :], jnp.zeros((half - reach, lanes), f32)], axis=0
        )
        for a in range(own)
    ]
    fold = lanes // half
    for g in range(0, own, fold):
        group = (around[g:g + fold] * fold)[:fold]
        t = jnp.transpose(jnp.concatenate(group, axis=0))
        for a in range(g, min(g + fold, own)):
            at = (a % fold) * half
            back = (lanes - at) % lanes

            def to_left(re, im):
                re = pltpu.roll(re, back, 1) if back else re
                im = pltpu.roll(im, (back + nvec) % lanes, 1) if (back + nvec) % lanes else im
                return jnp.where(left, jnp.where(real, re, im), 0.0)

            top = around[a] - to_left(t[:half], t[nvec:nvec + half])
            bottom = -to_left(t[half:nvec], t[nvec + half:])
            hi, lo = halves(jnp.concatenate([top, bottom], axis=0))
            dense_hl[a * nvec:(a + 1) * nvec, 0:lanes] = hi
            dense_hl[a * nvec:(a + 1) * nvec, lanes:2 * lanes] = lo

    for s in range(combos):
        at = s * 3 * lanes
        got = dot(dense_hl[...], right_hh[:, at:at + 3 * lanes]) + dot(
            dense_hl[:, 0:lanes], right_lo[:, at:at + 3 * lanes]
        )
        hi, lo = halves(got)
        for q in range(3):
            for a in range(own):
                where = (s * 3 + q, slice(None), pl.ds(a * lanes, lanes))
                half_hi[where] = hi[a * nvec:(a + 1) * nvec, q * lanes:(q + 1) * lanes]
                half_lo[where] = lo[a * nvec:(a + 1) * nvec, q * lanes:(q + 1) * lanes]
    for s in range(combos):
        for p in range(3):
            q, r = pairs[p]
            m = s * 3 + p
            r_hi = jnp.concatenate([half_hi[s * 3 + r], half_hi[s * 3 + q]], axis=0)
            r_lo = jnp.concatenate([half_lo[s * 3 + r], half_lo[s * 3 + q]], axis=0)
            got = dot(left_hl[m], jnp.concatenate([r_hi, r_hi], axis=0)) + dot(
                left_hl[m, :, 0:lanes], r_lo
            )
            for a in range(own):
                at = a * lanes
                whole = got[:nvec, at:at + lanes] + minus_plus * pltpu.roll(
                    got[nvec:, at:at + lanes], nvec, 1
                )
                rows = pl.ds((m * own + a) * half, half)
                cross_w[rows, :] = jnp.where(left, whole[half:], whole[:half])
                same_w[rows, :] = -0.5 * jnp.where(left, whole[:half], whole[half:])
    c_real = lax.broadcasted_iota(jnp.int32, (count, lanes), 1) < nvec
    for m in range(half // 2):
        even = same_w[pl.ds(2 * m, count, stride=half), :]
        odd = same_w[pl.ds(2 * m + 1, count, stride=half), :]
        re = jnp.where(c_real, even, pltpu.roll(odd, nvec, 1))
        im = jnp.where(c_real, pltpu.roll(even, nvec, 1), odd)
        at = pl.ds(m * lanes, lanes)
        for start, value in ((0, re), (low, im)):
            hi, lo = halves(value)
            lc_hi[start:start + count, at] = hi
            lc_lo[start:start + count, at] = lo

    for r in range(1, chips):
        own_copy(r).wait_recv()
        forward(r).start()
    own_copy(0).wait_recv()
    for r in range(1, chips):
        forward(r).wait_recv()
    for hf in range(2):
        at = hf * block_rows
        full[at:at + reach * reach, :] = full[at + half * reach:at + block_rows, :]

    inner = lax.broadcasted_iota(jnp.int32, (reach, lanes), 0)
    spot64 = lax.broadcasted_iota(jnp.int32, (nvec, lanes), 1) % nvec
    row64 = lax.broadcasted_iota(jnp.int32, (nvec, lanes), 0)
    crossing = (spot64 >= half) == (row64 < half)
    c_sign = jnp.where(c_real, -1.0, 1.0)
    mid = mid_ref[...]
    turned = pltpu.roll(mid, nvec, 1)
    pad = [jnp.zeros((low - count, nvec), jnp.bfloat16)] if low > count else []
    re_hi, re_lo = halves(mid[:, :nvec])
    im_hi, im_lo = halves(turned[:, :nvec])
    mid_hi = jnp.concatenate([re_hi] + pad + [im_hi], axis=0)
    mid_lo = jnp.concatenate([re_lo] + pad + [im_lo], axis=0)
    mid_k = jnp.concatenate([mid_hi, mid_hi, mid_lo], axis=1)
    one = jnp.zeros((count, lanes), f32)
    two = jnp.zeros((count, lanes), f32)
    for y in range(0, half, 2):
        pair = []
        for k in (y, y + 1):
            parts = []
            for hf in range(2):
                at = hf * block_rows
                before = full[pl.ds(at + reach * k + reach - 1, reach, stride=reach - 1), :]
                behind = full[pl.ds(at + reach * reach + reach * k - 1, reach), :]
                behind = jnp.where(inner == 0, 0.0, -behind)
                slab = jnp.concatenate([before, behind], axis=0)
                shift = (k - reach) % half
                if shift:
                    slab = pltpu.roll(slab, shift, 0)
                slabs[hf * half + k] = slab
                parts.append(slab)
            slab = jnp.concatenate(parts, axis=0)
            hi, lo = halves(slab)
            sl_hi[k * nvec:(k + 1) * nvec, :] = hi
            sl_lo[k * nvec:(k + 1) * nvec, :] = lo
            m_hi, m_lo = halves(jnp.where(crossing, slab, 0.0))
            pair.append(jnp.concatenate([m_hi, m_lo, m_hi], axis=0))
        got = dot(mid_k, jnp.concatenate(pair, axis=1))
        for b, k in enumerate((y, y + 1)):
            here = got[:, b * lanes:(b + 1) * lanes]
            value = here[:count] + c_sign * pltpu.roll(here[low:low + count], nvec, 1)
            weight = cross_w[pl.ds(k, count, stride=half), :]
            one = one + value * weight
            two = two + value * pltpu.roll(weight, nvec, 1)
    got = dot(lc_hi[...], sl_hi[...]) + (dot(lc_hi[...], sl_lo[...]) + dot(lc_lo[...], sl_hi[...]))
    value = got[:count] + c_sign * pltpu.roll(got[low:low + count], nvec, 1)
    one = one + value * mid
    two = two + value * turned
    one = jnp.where(c_real, one, -one)
    each = 3 * own
    tile_ref[...] = jnp.concatenate(
        [jnp.sum(one[s * each:(s + 1) * each], axis=0, keepdims=True) for s in range(combos)]
        + [jnp.sum(two[s * each:(s + 1) * each], axis=0, keepdims=True) for s in range(combos)],
        axis=0,
    )

    def sum_copy(r):
        return pltpu.make_async_remote_copy(
            tile_ref, box.at[r - 1], sum_send.at[r - 1], sum_recv.at[r - 1],
            device_id=(tm, (me + r) % n), device_id_type=MESH,
        )

    for r in range(1, n):
        sum_copy(r).start()

    for g in range(half // fold):
        t = jnp.transpose(jnp.concatenate(
            [slabs[other_side * half + g * fold + q] for q in range(fold)], axis=0
        ))
        turn[...] = t
        if own % 8 == 0:
            at = pl.multiple_of(side * half + first, own)
            pick[0, g * own:(g + 1) * own, :] = turn[pl.ds(at, own), :]
            pick[1, g * own:(g + 1) * own, :] = turn[pl.ds(at + nvec, own), :]
        else:
            for r in range(own):
                at = side * half + first + r
                pick[0, g * own + r:g * own + r + 1, :] = turn[pl.ds(at, 1), :]
                pick[1, g * own + r:g * own + r + 1, :] = turn[pl.ds(at + nvec, 1), :]
    steps = half // fold
    quarter = lax.broadcasted_iota(jnp.int32, (steps, lanes), 1) // half
    o_left = lax.broadcasted_iota(jnp.int32, (steps, lanes), 1) % nvec < half

    def shifted(x, by):
        by = by % lanes
        return pltpu.roll(x, by, 1) if by else x

    for g in range(0, own, fold):
        group = [slabs[side * half + first + a] for a in range(g, min(g + fold, own))]
        turn[...] = jnp.transpose(jnp.concatenate((group * fold)[:fold], axis=0))
        at = pl.multiple_of(other_side * half, half)
        re = turn[pl.ds(at, half), :]
        im = turn[pl.ds(at + nvec, half), :]
        turn[0:half, :] = re
        turn[half:2 * half, :] = im
        for a in range(g, min(g + fold, own)):
            for q in range(fold):
                x_re = turn[pl.ds(q, steps, stride=fold), :]
                x_im = turn[pl.ds(half + q, steps, stride=fold), :]
                c_re = pick[0, pl.ds(a, steps, stride=own), :]
                c_im = pick[1, pl.ds(a, steps, stride=own), :]
                back = (a % fold) * half
                value = jnp.where(
                    quarter < 2,
                    jnp.where(quarter == 0, -shifted(x_re, -back), shifted(c_re, half - q * half)),
                    jnp.where(quarter == 2, -shifted(x_im, nvec - back), shifted(c_im, nvec + half - q * half)),
                )
                flipped = jnp.where(o_left, pltpu.roll(value, lanes - half, 1), pltpu.roll(value, half, 1))
                value = jnp.where(side == 1, flipped, value)
                placed[pl.ds(q, steps, stride=fold), :] = value
            board[pl.ds(pl.multiple_of(side * half, half), half), :] = slabs[side * half + first + a]
            board[pl.ds(pl.multiple_of(other_side * half, half), half), :] = placed[0:half, :]
            even, odd = weave(board)
            out_ref[a, pl.ds(0, half, stride=2), :] = even
            out_ref[a, pl.ds(1, half, stride=2), :] = odd

    for s in range(chips):
        pair_copy(s).wait_send()
    for s in range(chips - 1):
        chip_copy(s).wait_send()
    for r in range(1, times):
        tm_copy(r).wait_send()
    own_copy(0).wait_send()
    for r in range(1, chips):
        own_copy(r).wait_send()
        forward(r).wait_send()
    answer = tile_ref[...]
    for r in range(1, n):
        sum_copy(r).wait_recv()
        answer = answer + box[r - 1]
    lines = jnp.sum(answer, axis=1, keepdims=True) * corr_scale
    corr_ref[...] = jnp.concatenate([lines[:combos], lines[combos:]], axis=1)
    for r in range(1, n):
        sum_copy(r).wait_send()


def shards(vectors, perambulators, shift_steps, spin_choice):
    vec = vectors[0]
    _, _, nvec, sites = vec.shape
    spin_pairs = perambulators.shape[1]
    combos = spin_choice.shape[0]
    n = lax.axis_size("space")
    times = lax.axis_size("tm")
    own, half, lanes = nvec // n, nvec // 2, 2 * nvec
    reach = half // 2
    wide = half + reach
    share = own * reach
    chips = n // 2
    count = combos * 3 * own
    low = -(-count // 16) * 16
    scale = 1.0 / math.sqrt(24.0 * sites * n)
    corr_scale = 0.25 / (nvec * math.sqrt(nvec))
    mats = perambulators[0].reshape(spin_pairs, 2, half, lanes)
    mats = jnp.transpose(mats, (0, 2, 1, 3)).reshape(spin_pairs, nvec, lanes)
    tile = (share, lanes)
    f32, bf16 = jnp.float32, jnp.bfloat16
    dma = pltpu.SemaphoreType.DMA
    smem = pl.BlockSpec(memory_space=pltpu.SMEM)
    out, correlator = pl.pallas_call(
        functools.partial(elementals_kernel, n, times, scale, corr_scale),
        out_shape=(
            jax.ShapeDtypeStruct((own, nvec, lanes), f32),
            jax.ShapeDtypeStruct((combos, 2), f32),
        ),
        in_specs=[VM, VM, smem, smem],
        out_specs=(VM, VM),
        scratch_shapes=[
            pltpu.VMEM((2, 3, 2 * wide, sites), f32),
            pltpu.VMEM((4 * nvec, 6 * sites), bf16),
            pltpu.VMEM((2 * share, 6 * sites), bf16),
            pltpu.VMEM((2 * share, 6 * sites), bf16),
            pltpu.VMEM((chips,) + tile, f32),
            pltpu.VMEM((chips,) + tile, f32),
            pltpu.VMEM((chips,) + tile, f32),
            pltpu.VMEM((chips - 1,) + tile, f32),
            pltpu.VMEM(tile, f32),
            pltpu.VMEM((2 * wide * reach, lanes), f32),
            pltpu.VMEM((times - 1,) + tile, f32),
            pltpu.VMEM((nvec, lanes), f32),
            pltpu.VMEM((combos, 3, nvec, lanes), f32),
            pltpu.VMEM((combos, 3, nvec, lanes), f32),
            pltpu.VMEM((2 * lanes, combos * 3 * lanes), bf16),
            pltpu.VMEM((lanes, combos * 3 * lanes), bf16),
            pltpu.VMEM((combos * 3, lanes, 2 * lanes), bf16),
            pltpu.VMEM((max(own, 2) * wide, lanes), f32),
            pltpu.VMEM((own * nvec, 2 * lanes), bf16),
            pltpu.VMEM((combos * 3, nvec, own * lanes), bf16),
            pltpu.VMEM((combos * 3, nvec, own * lanes), bf16),
            pltpu.VMEM((count * half, lanes), f32),
            pltpu.VMEM((count * half, lanes), f32),
            pltpu.VMEM((2 * low, half * nvec), bf16),
            pltpu.VMEM((2 * low, half * nvec), bf16),
            pltpu.VMEM((count, lanes), f32),
            pltpu.VMEM((nvec, half, lanes), f32),
            pltpu.VMEM((half * nvec, lanes), bf16),
            pltpu.VMEM((half * nvec, lanes), bf16),
            pltpu.VMEM((lanes, lanes), f32),
            pltpu.VMEM((2, own * (nvec // 8), lanes), f32),
            pltpu.VMEM((2 * combos, lanes), f32),
            pltpu.VMEM((n - 1, 2 * combos, lanes), f32),
            dma((chips,)), dma((chips,)),
            dma((chips - 1,)), dma((chips - 1,)),
            dma((chips,)), dma((chips,)),
            dma((chips - 1,)), dma((chips - 1,)),
            dma((times - 1,)), dma((times - 1,)),
            dma((n - 1,)), dma((n - 1,)),
        ],
        compiler_params=pltpu.CompilerParams(
            collective_id=0, has_side_effects=True, vmem_limit_bytes=60 * 1024 * 1024
        ),
        name="elementals",
    )(vec, mats, shift_steps, spin_choice)
    out = jnp.transpose(out.reshape(own, half, 2, lanes), (0, 2, 1, 3))
    return (out.reshape(1, own, 2, nvec * nvec), correlator[None])


def solution(mesh):
    placed = (P("tm", None, None, None, "space"), P("tm", None, None, None), P("tm"), P())
    return jax.shard_map(
        shards,
        mesh=mesh,
        in_specs=placed,
        out_specs=(P("tm", "space", None, None), P("tm", None, None)),
        check_vma=False,
    )
```

```python
import functools
import math

import jax
import jax.numpy as jnp
from jax import lax
from jax.experimental import pallas as pl
from jax.experimental.pallas import tpu as pltpu
from jax.sharding import PartitionSpec as P

MESH = pl.DeviceIdType.MESH
VM = pl.BlockSpec(memory_space=pltpu.VMEM)
NT_DIMS = (((1,), (1,)), ((), ()))


def halves(x):
    top = x.astype(jnp.bfloat16)
    return top, (x - top.astype(jnp.float32)).astype(jnp.bfloat16)


def dot(a, b):
    return jnp.dot(a, b, preferred_element_type=jnp.float32)


def elementals_kernel(
    n, times, scale, corr_scale, v_hbm, mats_hbm, shift_hbm, spin_ref, out_ref, corr_ref,
    v_ref, mats_ref, shift_ref, in_sem, vv, lead, d_hi, d_lo, keep, give, pair_in, chip_in, own_ref, full, sink_ref,
    board, spin_mats, local_mats, right_hh, right_lo, left_hl, placed, dense_hl,
    half_hi, half_lo, cross_w, same_w, lc_hi, lc_lo, mid_ref, slabs, sl_hi, sl_lo,
    turn, pick, tile_ref, box,
    pair_send, pair_recv, chip_send, chip_recv,
    own_send, own_recv, fwd_send, fwd_recv, tm_send, tm_recv,
    sum_send, sum_recv,
):
    f32 = jnp.float32
    me = lax.axis_index("space")
    tm = lax.axis_index("tm")
    chips = n // 2
    chip = me // 2
    core = me % 2
    mate = chip * 2 + 1 - core
    nvec = v_ref.shape[2]
    sites = v_ref.shape[3]
    own = nvec // n
    half = nvec // 2
    lanes = 2 * nvec
    reach = half // 2
    share = own * reach
    per_half = n // 2
    wide = half + reach
    block_rows = wide * reach
    side = me // per_half
    other_side = 1 - side
    first = (me % per_half) * own
    combos = spin_ref.shape[0]
    count = combos * 3 * own
    low = -(-count // 16) * 16

    def partner(m, back=False):
        if chips & (chips - 1):
            return (chip + chips - m) % chips if back else (chip + m) % chips
        out, bit = 0, 1
        while bit < chips:
            mine, its = chip // bit % 2, m // bit % 2
            out = out + bit * (mine + its - 2 * mine * its)
            bit *= 2
        return out

    barrier = pltpu.get_barrier_semaphore()
    for r in range(1, n):
        pl.semaphore_signal(barrier, inc=1, device_id=(tm, (me + r) % n), device_id_type=MESH)
    for r in range(1, times):
        pl.semaphore_signal(
            barrier, inc=1, device_id=((tm + r) % times, me), device_id_type=MESH
        )

    loads = [
        pltpu.make_async_copy(src, dst, in_sem.at[i])
        for i, (src, dst) in enumerate(((v_hbm, v_ref), (mats_hbm, mats_ref), (shift_hbm, shift_ref)))
    ]
    for load in loads:
        load.start()
    loads[0].wait()

    for a in range(3):
        re = v_ref[0, a]
        im = v_ref[1, a]
        re_hi, re_lo = halves(re)
        im_hi, im_lo = halves(im)
        one = pl.ds(a * sites, sites)
        two = pl.ds((3 + a) * sites, sites)
        lead[0:nvec, one] = re_hi
        lead[0:nvec, two] = -im_hi
        lead[nvec:lanes, one] = im_hi
        lead[nvec:lanes, two] = re_hi
        lead[lanes:lanes + nvec, one] = re_lo
        lead[lanes:lanes + nvec, two] = -im_lo
        lead[lanes + nvec:2 * lanes, one] = im_lo
        lead[lanes + nvec:2 * lanes, two] = re_lo
        for c, value in enumerate((re, im)):
            for hf in range(2):
                part = value[hf * half:(hf + 1) * half]
                for b in range(sites // 128):
                    cut = part[:, b * 128:(b + 1) * 128]
                    vv[c, a, b, pl.ds(2 * hf * wide, half, stride=2), :] = cut
                    vv[c, a, b, pl.ds(2 * (hf * wide + half), reach, stride=2), :] = cut[:reach]

    def fill(dest, slot, buf):
        base = (dest // per_half) * wide + (dest % per_half) * own
        for a in range(own):
            at = pl.ds(slot * share + a * reach, reach)
            for cut in range(sites // 128):
                mine = [[vv[c, x, cut, pl.ds(2 * (base + a), 1), :] for x in range(3)] for c in range(2)]
                other = [
                    [vv[c, x, cut, pl.ds(2 * (base + a + 1), reach, stride=2), :] for x in range(3)]
                    for c in range(2)
                ]
                for m in range(3):
                    b, d = (m + 1) % 3, (m + 2) % 3
                    real_part = (
                        mine[0][b] * other[0][d] - mine[1][b] * other[1][d]
                        - (mine[0][d] * other[0][b] - mine[1][d] * other[1][b])
                    )
                    imag_part = (
                        mine[0][b] * other[1][d] + mine[1][b] * other[0][d]
                        - (mine[0][d] * other[1][b] + mine[1][d] * other[0][b])
                    )
                    for q, value in ((m, real_part), (3 + m, imag_part)):
                        hi, lo = halves(value)
                        where = q * sites + cut * 128
                        d_hi[buf, at, where:where + 128] = hi
                        d_lo[buf, at, where:where + 128] = lo

    def pair_copy(s):
        return pltpu.make_async_remote_copy(
            give.at[s], pair_in.at[s], pair_send.at[s], pair_recv.at[s],
            device_id=(tm, mate), device_id_type=MESH,
        )

    def chip_copy(s):
        return pltpu.make_async_remote_copy(
            keep.at[s], chip_in.at[s], chip_send.at[s], chip_recv.at[s],
            device_id=(tm, partner(chips - 1 - s) * 2 + core), device_id_type=MESH,
        )

    def fills(s, buf):
        target = partner(chips - 1 - s) * 2
        fill(target + 1 - core, 0, buf)
        fill(target + core, 1, buf)

    def products(s, buf):
        both = lax.dot_general(d_hi[buf], lead[...], NT_DIMS, preferred_element_type=f32)
        rest = lax.dot_general(d_lo[buf], lead[0:lanes], NT_DIMS, preferred_element_type=f32)
        got = both[:, :lanes] + (both[:, lanes:] + rest)
        give[s] = got[:share]
        keep[s] = got[share:]

    def relay(s):
        pair_copy(s).wait_recv()
        keep[s] = keep[s] + pair_in[s]
        chip_copy(s).start()

    def one_chip(s, carry):
        fills(s, 0)
        products(s, 0)
        pair_copy(s).start()
        relay(s - 1)
        return carry

    fills(0, 0)
    if chips <= 4:
        for s in range(chips):
            products(s, s % 2)
            if s < chips - 1:
                fills(s + 1, (s + 1) % 2)
            if s == 0:
                pl.semaphore_wait(barrier, n - 1 + times - 1)
            pair_copy(s).start()
            if s:
                relay(s - 1)
    else:
        products(0, 0)
        pl.semaphore_wait(barrier, n - 1 + times - 1)
        pair_copy(0).start()
        lax.fori_loop(1, chips, one_chip, 0)

    lane = lax.broadcasted_iota(jnp.int32, (half, lanes), 1)
    spot = lane % nvec
    left = spot < half
    real = lane < nvec
    minus_plus = jnp.where(lax.broadcasted_iota(jnp.int32, (nvec, lanes), 1) < nvec, -1.0, 1.0)

    def weave(ref):
        even = ref[pl.ds(0, half, stride=2), :]
        odd = ref[pl.ds(1, half, stride=2), :]
        return (
            jnp.where(real, even, pltpu.roll(odd, nvec, 1)),
            jnp.where(real, pltpu.roll(even, nvec, 1), odd),
        )

    loads[1].wait()
    loads[2].wait()
    for s in range(combos):
        for q in range(3):
            board[...] = mats_ref[spin_ref[s, q]]
            even, odd = weave(board)
            spin_mats[s, q, pl.ds(0, half, stride=2), :] = even
            spin_mats[s, q, pl.ds(1, half, stride=2), :] = odd
            near = spin_mats[s, q, pl.ds(pl.multiple_of(side * half, half), half), :]
            far = spin_mats[s, q, pl.ds(pl.multiple_of(other_side * half, half), half), :]
            local = jnp.concatenate([near, far], axis=0)
            local_mats[s, q] = local
            at = (s * 3 + q) * lanes
            top_hi, top_lo = halves(local)
            low_hi, low_lo = halves(minus_plus * pltpu.roll(local, nvec, 1))
            right_hh[0:nvec, at:at + lanes] = top_hi
            right_hh[nvec:lanes, at:at + lanes] = low_hi
            right_hh[lanes:lanes + nvec, at:at + lanes] = top_hi
            right_hh[lanes + nvec:2 * lanes, at:at + lanes] = low_hi
            right_lo[0:nvec, at:at + lanes] = top_lo
            right_lo[nvec:lanes, at:at + lanes] = low_lo
    pairs = ((1, 2), (0, 2), (0, 1))
    for s in range(combos):
        for p in range(3):
            q, r = pairs[p]
            both = jnp.transpose(jnp.concatenate([local_mats[s, q], local_mats[s, r]], axis=0))
            hi, lo = halves(both)
            left_hl[s * 3 + p, :, 0:lanes] = hi
            left_hl[s * 3 + p, :, lanes:2 * lanes] = lo
    for s in range(combos):
        for p in range(3):
            if own % 8 == 0:
                rows = spin_mats[s, p, pl.ds(pl.multiple_of(me * own, own), own), :]
                mid_ref[(s * 3 + p) * own:(s * 3 + p + 1) * own, :] = rows
            else:
                for r in range(own):
                    at = (s * 3 + p) * own + r
                    mid_ref[at:at + 1, :] = spin_mats[s, p, pl.ds(me * own + r, 1), :]

    last = chips - 1
    pair_copy(last).wait_recv()
    total = keep[last] + pair_in[last]
    for s in range(last):
        chip_copy(s).wait_recv()
        total = total + chip_in[s]
    own_ref[...] = total * scale

    def rows_of(d):
        start = (d // per_half) * block_rows + reach * reach + (d % per_half) * share
        return pl.ds(pl.multiple_of(start, reach), share)

    def tm_copy(r):
        return pltpu.make_async_remote_copy(
            own_ref, sink_ref.at[r - 1], tm_send.at[r - 1], tm_recv.at[r - 1],
            device_id=((tm + r) % times, me), device_id_type=MESH,
        )

    def own_copy(r):
        target = mate if r == 0 else partner(r) * 2 + core
        return pltpu.make_async_remote_copy(
            own_ref, full.at[rows_of(me)], own_send.at[r], own_recv.at[r],
            device_id=(tm, target), device_id_type=MESH,
        )

    def forward(r):
        at = rows_of(partner(r, True) * 2 + core)
        return pltpu.make_async_remote_copy(
            full.at[at], full.at[at], fwd_send.at[r - 1], fwd_recv.at[r - 1],
            device_id=(tm, mate), device_id_type=MESH,
        )

    for r in range(1, times):
        tm_copy(r).start()
    for r in range(chips - 1, 0, -1):
        own_copy(r).start()
    own_copy(0).start()
    full[rows_of(me), :] = own_ref[...]

    for r in range(1, times):
        tm_copy(r).wait_recv()
    chosen = sink_ref[jnp.clip(times - 1 - shift_ref[0], 0, times - 2)]
    wide_lane = lax.broadcasted_iota(jnp.int32, (share, lanes), 1)
    wide_left = wide_lane % nvec < half
    swapped = jnp.where(wide_left, pltpu.roll(chosen, lanes - half, 1), pltpu.roll(chosen, half, 1))
    chosen = jnp.where(side == 1, swapped, chosen)
    step_of = lax.broadcasted_iota(jnp.int32, (share, lanes), 0) % reach
    factor = jnp.where(wide_left, 1.0 / 3.0, 1.0) * jnp.where(step_of == reach - 1, 0.5, 1.0)
    chosen = chosen * jnp.where(wide_lane < nvec, factor, -factor)
    placed[...] = jnp.zeros_like(placed)
    for a in range(own):
        if own % 8 == 0:
            start = pl.multiple_of(a * wide + first, 8)
            view = placed.at[pl.ds(start, own + reach), :]
            view[a + 1:a + 1 + reach, :] = chosen[a * reach:(a + 1) * reach]
        else:
            for r in range(reach):
                at = a * wide + first + a + 1 + r
                placed[pl.ds(at, 1), :] = chosen[a * reach + r:a * reach + r + 1]
    around = [
        placed[a * wide:a * wide + half, :] + jnp.concatenate(
            [placed[a * wide + half:(a + 1) * wide, :], jnp.zeros((half - reach, lanes), f32)], axis=0
        )
        for a in range(own)
    ]
    fold = lanes // half
    for g in range(0, own, fold):
        group = (around[g:g + fold] * fold)[:fold]
        t = jnp.transpose(jnp.concatenate(group, axis=0))
        for a in range(g, min(g + fold, own)):
            at = (a % fold) * half
            back = (lanes - at) % lanes

            def to_left(re, im):
                re = pltpu.roll(re, back, 1) if back else re
                im = pltpu.roll(im, (back + nvec) % lanes, 1) if (back + nvec) % lanes else im
                return jnp.where(left, jnp.where(real, re, im), 0.0)

            top = around[a] - to_left(t[:half], t[nvec:nvec + half])
            bottom = -to_left(t[half:nvec], t[nvec + half:])
            hi, lo = halves(jnp.concatenate([top, bottom], axis=0))
            dense_hl[a * nvec:(a + 1) * nvec, 0:lanes] = hi
            dense_hl[a * nvec:(a + 1) * nvec, lanes:2 * lanes] = lo

    for s in range(combos):
        at = s * 3 * lanes
        got = dot(dense_hl[...], right_hh[:, at:at + 3 * lanes]) + dot(
            dense_hl[:, 0:lanes], right_lo[:, at:at + 3 * lanes]
        )
        hi, lo = halves(got)
        for q in range(3):
            for a in range(own):
                where = (s * 3 + q, slice(None), pl.ds(a * lanes, lanes))
                half_hi[where] = hi[a * nvec:(a + 1) * nvec, q * lanes:(q + 1) * lanes]
                half_lo[where] = lo[a * nvec:(a + 1) * nvec, q * lanes:(q + 1) * lanes]
    for s in range(combos):
        for p in range(3):
            q, r = pairs[p]
            m = s * 3 + p
            r_hi = jnp.concatenate([half_hi[s * 3 + r], half_hi[s * 3 + q]], axis=0)
            r_lo = jnp.concatenate([half_lo[s * 3 + r], half_lo[s * 3 + q]], axis=0)
            got = dot(left_hl[m], jnp.concatenate([r_hi, r_hi], axis=0)) + dot(
                left_hl[m, :, 0:lanes], r_lo
            )
            for a in range(own):
                at = a * lanes
                whole = got[:nvec, at:at + lanes] + minus_plus * pltpu.roll(
                    got[nvec:, at:at + lanes], nvec, 1
                )
                rows = pl.ds((m * own + a) * half, half)
                cross_w[rows, :] = jnp.where(left, whole[half:], whole[:half])
                same_w[rows, :] = -0.5 * jnp.where(left, whole[:half], whole[half:])
    for r in range(1, chips):
        own_copy(r).wait_recv()
        forward(r).start()
    c_real = lax.broadcasted_iota(jnp.int32, (count, lanes), 1) < nvec
    for m in range(half // 2):
        even = same_w[pl.ds(2 * m, count, stride=half), :]
        odd = same_w[pl.ds(2 * m + 1, count, stride=half), :]
        re = jnp.where(c_real, even, pltpu.roll(odd, nvec, 1))
        im = jnp.where(c_real, pltpu.roll(even, nvec, 1), odd)
        at = pl.ds(m * lanes, lanes)
        for start, value in ((0, re), (low, im)):
            hi, lo = halves(value)
            lc_hi[start:start + count, at] = hi
            lc_lo[start:start + count, at] = lo

    own_copy(0).wait_recv()
    for r in range(1, chips):
        forward(r).wait_recv()
    for hf in range(2):
        at = hf * block_rows
        full[at:at + reach * reach, :] = full[at + half * reach:at + block_rows, :]

    inner = lax.broadcasted_iota(jnp.int32, (reach, lanes), 0)
    spot64 = lax.broadcasted_iota(jnp.int32, (nvec, lanes), 1) % nvec
    row64 = lax.broadcasted_iota(jnp.int32, (nvec, lanes), 0)
    crossing = (spot64 >= half) == (row64 < half)
    c_sign = jnp.where(c_real, -1.0, 1.0)
    mid = mid_ref[...]
    turned = pltpu.roll(mid, nvec, 1)
    pad = [jnp.zeros((low - count, nvec), jnp.bfloat16)] if low > count else []
    re_hi, re_lo = halves(mid[:, :nvec])
    im_hi, im_lo = halves(turned[:, :nvec])
    mid_hi = jnp.concatenate([re_hi] + pad + [im_hi], axis=0)
    mid_lo = jnp.concatenate([re_lo] + pad + [im_lo], axis=0)
    mid_k = jnp.concatenate([mid_hi, mid_hi, mid_lo], axis=1)
    one = jnp.zeros((count, lanes), f32)
    two = jnp.zeros((count, lanes), f32)
    for y in range(0, half, 2):
        pair = []
        for k in (y, y + 1):
            parts = []
            for hf in range(2):
                at = hf * block_rows
                before = full[pl.ds(at + reach * k + reach - 1, reach, stride=reach - 1), :]
                behind = full[pl.ds(at + reach * reach + reach * k - 1, reach), :]
                behind = jnp.where(inner == 0, 0.0, -behind)
                slab = jnp.concatenate([before, behind], axis=0)
                shift = (k - reach) % half
                if shift:
                    slab = pltpu.roll(slab, shift, 0)
                slabs[hf * half + k] = slab
                parts.append(slab)
            slab = jnp.concatenate(parts, axis=0)
            hi, lo = halves(slab)
            sl_hi[k * nvec:(k + 1) * nvec, :] = hi
            sl_lo[k * nvec:(k + 1) * nvec, :] = lo
            m_hi, m_lo = halves(jnp.where(crossing, slab, 0.0))
            pair.append(jnp.concatenate([m_hi, m_lo, m_hi], axis=0))
        got = dot(mid_k, jnp.concatenate(pair, axis=1))
        for b, k in enumerate((y, y + 1)):
            here = got[:, b * lanes:(b + 1) * lanes]
            value = here[:count] + c_sign * pltpu.roll(here[low:low + count], nvec, 1)
            weight = cross_w[pl.ds(k, count, stride=half), :]
            one = one + value * weight
            two = two + value * pltpu.roll(weight, nvec, 1)
    got = dot(lc_hi[...], sl_hi[...]) + (dot(lc_hi[...], sl_lo[...]) + dot(lc_lo[...], sl_hi[...]))
    value = got[:count] + c_sign * pltpu.roll(got[low:low + count], nvec, 1)
    one = one + value * mid
    two = two + value * turned
    one = jnp.where(c_real, one, -one)
    each = 3 * own
    tile_ref[...] = jnp.concatenate(
        [jnp.sum(one[s * each:(s + 1) * each], axis=0, keepdims=True) for s in range(combos)]
        + [jnp.sum(two[s * each:(s + 1) * each], axis=0, keepdims=True) for s in range(combos)],
        axis=0,
    )

    def sum_copy(r):
        return pltpu.make_async_remote_copy(
            tile_ref, box.at[r - 1], sum_send.at[r - 1], sum_recv.at[r - 1],
            device_id=(tm, (me + r) % n), device_id_type=MESH,
        )

    for r in range(1, n):
        sum_copy(r).start()

    for g in range(half // fold):
        t = jnp.transpose(jnp.concatenate(
            [slabs[other_side * half + g * fold + q] for q in range(fold)], axis=0
        ))
        turn[...] = t
        if own % 8 == 0:
            at = pl.multiple_of(side * half + first, own)
            pick[0, g * own:(g + 1) * own, :] = turn[pl.ds(at, own), :]
            pick[1, g * own:(g + 1) * own, :] = turn[pl.ds(at + nvec, own), :]
        else:
            for r in range(own):
                at = side * half + first + r
                pick[0, g * own + r:g * own + r + 1, :] = turn[pl.ds(at, 1), :]
                pick[1, g * own + r:g * own + r + 1, :] = turn[pl.ds(at + nvec, 1), :]
    steps = half // fold
    quarter = lax.broadcasted_iota(jnp.int32, (steps, lanes), 1) // half
    o_left = lax.broadcasted_iota(jnp.int32, (steps, lanes), 1) % nvec < half

    def shifted(x, by):
        by = by % lanes
        return pltpu.roll(x, by, 1) if by else x

    for g in range(0, own, fold):
        group = [slabs[side * half + first + a] for a in range(g, min(g + fold, own))]
        turn[...] = jnp.transpose(jnp.concatenate((group * fold)[:fold], axis=0))
        at = pl.multiple_of(other_side * half, half)
        re = turn[pl.ds(at, half), :]
        im = turn[pl.ds(at + nvec, half), :]
        turn[0:half, :] = re
        turn[half:2 * half, :] = im
        for a in range(g, min(g + fold, own)):
            for q in range(fold):
                x_re = turn[pl.ds(q, steps, stride=fold), :]
                x_im = turn[pl.ds(half + q, steps, stride=fold), :]
                c_re = pick[0, pl.ds(a, steps, stride=own), :]
                c_im = pick[1, pl.ds(a, steps, stride=own), :]
                back = (a % fold) * half
                value = jnp.where(
                    quarter < 2,
                    jnp.where(quarter == 0, -shifted(x_re, -back), shifted(c_re, half - q * half)),
                    jnp.where(quarter == 2, -shifted(x_im, nvec - back), shifted(c_im, nvec + half - q * half)),
                )
                flipped = jnp.where(o_left, pltpu.roll(value, lanes - half, 1), pltpu.roll(value, half, 1))
                value = jnp.where(side == 1, flipped, value)
                placed[pl.ds(q, steps, stride=fold), :] = value
            board[pl.ds(pl.multiple_of(side * half, half), half), :] = slabs[side * half + first + a]
            board[pl.ds(pl.multiple_of(other_side * half, half), half), :] = placed[0:half, :]
            even, odd = weave(board)
            out_ref[a, pl.ds(0, half, stride=2), :] = even
            out_ref[a, pl.ds(1, half, stride=2), :] = odd

    for s in range(chips):
        pair_copy(s).wait_send()
    for s in range(chips - 1):
        chip_copy(s).wait_send()
    for r in range(1, times):
        tm_copy(r).wait_send()
    own_copy(0).wait_send()
    for r in range(1, chips):
        own_copy(r).wait_send()
        forward(r).wait_send()
    answer = tile_ref[...]
    for r in range(1, n):
        sum_copy(r).wait_recv()
        answer = answer + box[r - 1]
    total = jnp.sum(jnp.transpose(answer), axis=0, keepdims=True) * corr_scale
    corr_ref[...] = jnp.concatenate([total[:, :combos], total[:, combos:]], axis=0)
    for r in range(1, n):
        sum_copy(r).wait_send()


def shards(vectors, perambulators, shift_steps, spin_choice):
    vec = vectors[0]
    _, _, nvec, sites = vec.shape
    spin_pairs = perambulators.shape[1]
    combos = spin_choice.shape[0]
    n = lax.axis_size("space")
    times = lax.axis_size("tm")
    own, half, lanes = nvec // n, nvec // 2, 2 * nvec
    reach = half // 2
    wide = half + reach
    share = own * reach
    chips = n // 2
    count = combos * 3 * own
    low = -(-count // 16) * 16
    scale = 1.0 / math.sqrt(24.0 * sites * n)
    corr_scale = 0.25 / (nvec * math.sqrt(nvec))
    mats = perambulators[0].reshape(spin_pairs, 2, half, lanes)
    mats = jnp.transpose(mats, (0, 2, 1, 3)).reshape(spin_pairs, nvec, lanes)
    tile = (share, lanes)
    f32, bf16 = jnp.float32, jnp.bfloat16
    dma = pltpu.SemaphoreType.DMA
    smem = pl.BlockSpec(memory_space=pltpu.SMEM)
    anywhere = pl.BlockSpec(memory_space=pl.ANY)
    out, correlator = pl.pallas_call(
        functools.partial(elementals_kernel, n, times, scale, corr_scale),
        out_shape=(
            pltpu.VMEM((own, nvec, lanes), f32),
            pltpu.VMEM((2, combos), f32),
        ),
        in_specs=[anywhere, anywhere, anywhere, smem],
        out_specs=(VM, VM),
        scratch_shapes=[
            pltpu.VMEM(vec.shape, f32),
            pltpu.VMEM(mats.shape, f32),
            pltpu.SMEM(shift_steps.shape, jnp.int32),
            dma((3,)),
            pltpu.VMEM((2, 3, sites // 128, 4 * wide, 128), f32),
            pltpu.VMEM((4 * nvec, 6 * sites), bf16),
            pltpu.VMEM((2, 2 * share, 6 * sites), bf16),
            pltpu.VMEM((2, 2 * share, 6 * sites), bf16),
            pltpu.VMEM((chips,) + tile, f32),
            pltpu.VMEM((chips,) + tile, f32),
            pltpu.VMEM((chips,) + tile, f32),
            pltpu.VMEM((chips - 1,) + tile, f32),
            pltpu.VMEM(tile, f32),
            pltpu.VMEM((2 * wide * reach, lanes), f32),
            pltpu.VMEM((times - 1,) + tile, f32),
            pltpu.VMEM((nvec, lanes), f32),
            pltpu.VMEM((combos, 3, nvec, lanes), f32),
            pltpu.VMEM((combos, 3, nvec, lanes), f32),
            pltpu.VMEM((2 * lanes, combos * 3 * lanes), bf16),
            pltpu.VMEM((lanes, combos * 3 * lanes), bf16),
            pltpu.VMEM((combos * 3, lanes, 2 * lanes), bf16),
            pltpu.VMEM((max(own, 2) * wide, lanes), f32),
            pltpu.VMEM((own * nvec, 2 * lanes), bf16),
            pltpu.VMEM((combos * 3, nvec, own * lanes), bf16),
            pltpu.VMEM((combos * 3, nvec, own * lanes), bf16),
            pltpu.VMEM((count * half, lanes), f32),
            pltpu.VMEM((count * half, lanes), f32),
            pltpu.VMEM((2 * low, half * nvec), bf16),
            pltpu.VMEM((2 * low, half * nvec), bf16),
            pltpu.VMEM((count, lanes), f32),
            pltpu.VMEM((nvec, half, lanes), f32),
            pltpu.VMEM((half * nvec, lanes), bf16),
            pltpu.VMEM((half * nvec, lanes), bf16),
            pltpu.VMEM((lanes, lanes), f32),
            pltpu.VMEM((2, own * (nvec // 8), lanes), f32),
            pltpu.VMEM((2 * combos, lanes), f32),
            pltpu.VMEM((n - 1, 2 * combos, lanes), f32),
            dma((chips,)), dma((chips,)),
            dma((chips - 1,)), dma((chips - 1,)),
            dma((chips,)), dma((chips,)),
            dma((chips - 1,)), dma((chips - 1,)),
            dma((times - 1,)), dma((times - 1,)),
            dma((n - 1,)), dma((n - 1,)),
        ],
        compiler_params=pltpu.CompilerParams(
            collective_id=0, has_side_effects=True, vmem_limit_bytes=60 * 1024 * 1024
        ),
        name="elementals",
    )(vec, mats, shift_steps, spin_choice)
    out = jnp.transpose(out.reshape(own, half, 2, lanes), (0, 2, 1, 3))
    return (out.reshape(1, own, 2, nvec * nvec), jnp.transpose(correlator)[None])


def solution(mesh):
    placed = (P("tm", None, None, None, "space"), P("tm", None, None, None), P("tm"), P())
    return jax.shard_map(
        shards,
        mesh=mesh,
        in_specs=placed,
        out_specs=(P("tm", "space", None, None), P("tm", None, None)),
        check_vma=False,
    )
```

```python
import functools
import math

import jax
import jax.numpy as jnp
from jax import lax
from jax.experimental import pallas as pl
from jax.experimental.pallas import tpu as pltpu
from jax.sharding import PartitionSpec as P

MESH = pl.DeviceIdType.MESH
VM = pl.BlockSpec(memory_space=pltpu.VMEM)
NT_DIMS = (((1,), (1,)), ((), ()))


def halves(x):
    top = x.astype(jnp.bfloat16)
    return top, (x - top.astype(jnp.float32)).astype(jnp.bfloat16)


def dot(a, b):
    return jnp.dot(a, b, preferred_element_type=jnp.float32)


def elementals_kernel(
    n, times, scale, corr_scale, v_hbm, mats_hbm, shift_hbm, spin_ref, out_ref, corr_ref,
    v_ref, mats_ref, shift_ref, in_sem, vv, lead, d_hi, d_lo, keep, give, pair_in, chip_in, own_ref, full, sink_ref,
    board, spin_mats, local_mats, right_hl, left_hl, placed, dense_hh, dense_lo,
    inner_ref, inner_hi, inner_lo, cross_w, same_w, lc_hi, lc_lo, mid_ref, slabs, sl_hl,
    turn, pick, tile_ref, box,
    pair_send, pair_recv, chip_send, chip_recv,
    own_send, own_recv, fwd_send, fwd_recv, tm_send, tm_recv,
    sum_send, sum_recv,
):
    f32 = jnp.float32
    me = lax.axis_index("space")
    tm = lax.axis_index("tm")
    chips = n // 2
    chip = me // 2
    core = me % 2
    mate = chip * 2 + 1 - core
    nvec = v_ref.shape[2]
    sites = v_ref.shape[3]
    own = nvec // n
    half = nvec // 2
    lanes = 2 * nvec
    reach = half // 2
    share = own * reach
    per_half = n // 2
    wide = half + reach
    block_rows = wide * reach
    side = me // per_half
    other_side = 1 - side
    first = (me % per_half) * own
    combos = spin_ref.shape[0]
    count = combos * 3 * own
    low = -(-count // 16) * 16

    def partner(m, back=False):
        if chips & (chips - 1):
            return (chip + chips - m) % chips if back else (chip + m) % chips
        out, bit = 0, 1
        while bit < chips:
            mine, its = chip // bit % 2, m // bit % 2
            out = out + bit * (mine + its - 2 * mine * its)
            bit *= 2
        return out

    barrier = pltpu.get_barrier_semaphore()
    for r in range(1, n):
        pl.semaphore_signal(barrier, inc=1, device_id=(tm, (me + r) % n), device_id_type=MESH)
    for r in range(1, times):
        pl.semaphore_signal(
            barrier, inc=1, device_id=((tm + r) % times, me), device_id_type=MESH
        )

    vec_loads = [
        [
            pltpu.make_async_copy(v_hbm.at[c, a], v_ref.at[c, a], in_sem.at[c * 3 + a])
            for a in range(3)
        ]
        for c in range(2)
    ]
    mat_load = pltpu.make_async_copy(mats_hbm, mats_ref, in_sem.at[6])
    shift_load = pltpu.make_async_copy(shift_hbm, shift_ref, in_sem.at[7])
    for a in range(3):
        vec_loads[0][a].start()
        vec_loads[1][a].start()

    for a in range(3):
        vec_loads[0][a].wait()
        vec_loads[1][a].wait()
        re = v_ref[0, a]
        im = v_ref[1, a]
        re_hi, re_lo = halves(re)
        im_hi, im_lo = halves(im)
        one = pl.ds(a * sites, sites)
        two = pl.ds((3 + a) * sites, sites)
        lead[0:nvec, one] = re_hi
        lead[0:nvec, two] = -im_hi
        lead[nvec:lanes, one] = im_hi
        lead[nvec:lanes, two] = re_hi
        lead[lanes:lanes + nvec, one] = re_lo
        lead[lanes:lanes + nvec, two] = -im_lo
        lead[lanes + nvec:2 * lanes, one] = im_lo
        lead[lanes + nvec:2 * lanes, two] = re_lo
        for c, value in enumerate((re, im)):
            for hf in range(2):
                part = value[hf * half:(hf + 1) * half]
                for b in range(sites // 128):
                    cut = part[:, b * 128:(b + 1) * 128]
                    vv[c, a, b, pl.ds(2 * hf * wide, half, stride=2), :] = cut
                    vv[c, a, b, pl.ds(2 * (hf * wide + half), reach, stride=2), :] = cut[:reach]

    mat_load.start()
    shift_load.start()

    def fill(dest, slot, buf):
        base = (dest // per_half) * wide + (dest % per_half) * own
        for a in range(own):
            at = pl.ds(slot * share + a * reach, reach)
            for cut in range(sites // 128):
                mine = [[vv[c, x, cut, pl.ds(2 * (base + a), 1), :] for x in range(3)] for c in range(2)]
                other = [
                    [vv[c, x, cut, pl.ds(2 * (base + a + 1), reach, stride=2), :] for x in range(3)]
                    for c in range(2)
                ]
                for m in range(3):
                    b, d = (m + 1) % 3, (m + 2) % 3
                    real_part = (
                        mine[0][b] * other[0][d] - mine[1][b] * other[1][d]
                        - (mine[0][d] * other[0][b] - mine[1][d] * other[1][b])
                    )
                    imag_part = (
                        mine[0][b] * other[1][d] + mine[1][b] * other[0][d]
                        - (mine[0][d] * other[1][b] + mine[1][d] * other[0][b])
                    )
                    for q, value in ((m, real_part), (3 + m, imag_part)):
                        hi, lo = halves(value)
                        where = q * sites + cut * 128
                        d_hi[buf, at, where:where + 128] = hi
                        d_lo[buf, at, where:where + 128] = lo

    def pair_copy(s):
        return pltpu.make_async_remote_copy(
            give.at[s], pair_in.at[s], pair_send.at[s], pair_recv.at[s],
            device_id=(tm, mate), device_id_type=MESH,
        )

    def chip_copy(s):
        return pltpu.make_async_remote_copy(
            keep.at[s], chip_in.at[s], chip_send.at[s], chip_recv.at[s],
            device_id=(tm, partner(chips - 1 - s) * 2 + core), device_id_type=MESH,
        )

    def fills(s, buf):
        target = partner(chips - 1 - s) * 2
        fill(target + 1 - core, 0, buf)
        fill(target + core, 1, buf)

    def products(s, buf):
        both = lax.dot_general(d_hi[buf], lead[...], NT_DIMS, preferred_element_type=f32)
        rest = lax.dot_general(d_lo[buf], lead[0:lanes], NT_DIMS, preferred_element_type=f32)
        got = both[:, :lanes] + (both[:, lanes:] + rest)
        give[s] = got[:share]
        keep[s] = got[share:]

    def relay(s):
        pair_copy(s).wait_recv()
        keep[s] = keep[s] + pair_in[s]
        chip_copy(s).start()

    def one_chip(s, carry):
        fills(s, 0)
        products(s, 0)
        pair_copy(s).start()
        relay(s - 1)
        return carry

    fills(0, 0)
    if chips <= 4:
        for s in range(chips):
            products(s, s % 2)
            if s < chips - 1:
                fills(s + 1, (s + 1) % 2)
            if s == 0:
                pl.semaphore_wait(barrier, n - 1 + times - 1)
            pair_copy(s).start()
            if s:
                relay(s - 1)
    else:
        products(0, 0)
        pl.semaphore_wait(barrier, n - 1 + times - 1)
        pair_copy(0).start()
        lax.fori_loop(1, chips, one_chip, 0)

    lane = lax.broadcasted_iota(jnp.int32, (half, lanes), 1)
    spot = lane % nvec
    left = spot < half
    real = lane < nvec
    minus_plus = jnp.where(lax.broadcasted_iota(jnp.int32, (nvec, lanes), 1) < nvec, -1.0, 1.0)

    def weave(ref):
        even = ref[pl.ds(0, half, stride=2), :]
        odd = ref[pl.ds(1, half, stride=2), :]
        return (
            jnp.where(real, even, pltpu.roll(odd, nvec, 1)),
            jnp.where(real, pltpu.roll(even, nvec, 1), odd),
        )

    pairs = ((1, 2), (0, 2), (0, 1))
    mat_load.wait()
    shift_load.wait()
    for s in range(combos):
        for q in range(3):
            board[...] = mats_ref[spin_ref[s, q]]
            even, odd = weave(board)
            spin_mats[s, q, pl.ds(0, half, stride=2), :] = even
            spin_mats[s, q, pl.ds(1, half, stride=2), :] = odd
            near = spin_mats[s, q, pl.ds(pl.multiple_of(side * half, half), half), :]
            far = spin_mats[s, q, pl.ds(pl.multiple_of(other_side * half, half), half), :]
            local = jnp.concatenate([near, far], axis=0)
            local_mats[s, q] = local
            parts = halves(local) + halves(minus_plus * pltpu.roll(local, nvec, 1))
            for p in range(3):
                if q in pairs[p]:
                    at = pairs[p].index(q) * lanes
                    for row, top, low_part in ((0, parts[0], parts[2]), (lanes, parts[1], parts[3])):
                        right_hl[s * 3 + p, at:at + nvec, row:row + lanes] = top
                        right_hl[s * 3 + p, at + nvec:at + lanes, row:row + lanes] = low_part
    flat = [(s, q) for s in range(combos) for q in range(3)]
    wide_real = lax.broadcasted_iota(jnp.int32, (nvec, lanes), 1) < nvec
    for m in range(0, len(flat), 2):
        ahead = flat[m + 1] if m + 1 < len(flat) else flat[m]
        t = jnp.transpose(jnp.concatenate([local_mats[flat[m]], local_mats[ahead]], axis=0))
        up, down = t[:nvec], t[nvec:]
        here = jnp.where(wide_real, up, pltpu.roll(down, nvec, 1))
        there = jnp.where(wide_real, pltpu.roll(up, nvec, 1), down)
        for k, value in ((m, here), (m + 1, there)):
            if k < len(flat):
                hi, lo = halves(value)
                left_hl[k * nvec:(k + 1) * nvec, 0:lanes] = hi
                left_hl[k * nvec:(k + 1) * nvec, lanes:2 * lanes] = lo
    for s in range(combos):
        for p in range(3):
            if own % 8 == 0:
                rows = spin_mats[s, p, pl.ds(pl.multiple_of(me * own, own), own), :]
                mid_ref[(s * 3 + p) * own:(s * 3 + p + 1) * own, :] = rows
            else:
                for r in range(own):
                    at = (s * 3 + p) * own + r
                    mid_ref[at:at + 1, :] = spin_mats[s, p, pl.ds(me * own + r, 1), :]

    last = chips - 1
    pair_copy(last).wait_recv()
    total = keep[last] + pair_in[last]
    for s in range(last):
        chip_copy(s).wait_recv()
        total = total + chip_in[s]
    own_ref[...] = total * scale

    def rows_of(d):
        start = (d // per_half) * block_rows + reach * reach + (d % per_half) * share
        return pl.ds(pl.multiple_of(start, reach), share)

    def tm_copy(r):
        return pltpu.make_async_remote_copy(
            own_ref, sink_ref.at[r - 1], tm_send.at[r - 1], tm_recv.at[r - 1],
            device_id=((tm + r) % times, me), device_id_type=MESH,
        )

    def own_copy(r):
        target = mate if r == 0 else partner(r) * 2 + core
        return pltpu.make_async_remote_copy(
            own_ref, full.at[rows_of(me)], own_send.at[r], own_recv.at[r],
            device_id=(tm, target), device_id_type=MESH,
        )

    def forward(r):
        at = rows_of(partner(r, True) * 2 + core)
        return pltpu.make_async_remote_copy(
            full.at[at], full.at[at], fwd_send.at[r - 1], fwd_recv.at[r - 1],
            device_id=(tm, mate), device_id_type=MESH,
        )

    for r in range(1, times):
        tm_copy(r).start()
    for r in range(chips - 1, 0, -1):
        own_copy(r).start()
    own_copy(0).start()
    full[rows_of(me), :] = own_ref[...]

    for r in range(1, times):
        tm_copy(r).wait_recv()
    chosen = sink_ref[jnp.clip(times - 1 - shift_ref[0], 0, times - 2)]
    wide_lane = lax.broadcasted_iota(jnp.int32, (share, lanes), 1)
    wide_left = wide_lane % nvec < half
    swapped = jnp.where(wide_left, pltpu.roll(chosen, lanes - half, 1), pltpu.roll(chosen, half, 1))
    chosen = jnp.where(side == 1, swapped, chosen)
    step_of = lax.broadcasted_iota(jnp.int32, (share, lanes), 0) % reach
    factor = jnp.where(wide_left, 1.0 / 3.0, 1.0) * jnp.where(step_of == reach - 1, 0.5, 1.0)
    chosen = chosen * jnp.where(wide_lane < nvec, factor, -factor)
    placed[...] = jnp.zeros_like(placed)
    for a in range(own):
        if own % 8 == 0:
            start = pl.multiple_of(a * wide + first, 8)
            view = placed.at[pl.ds(start, own + reach), :]
            view[a + 1:a + 1 + reach, :] = chosen[a * reach:(a + 1) * reach]
        else:
            for r in range(reach):
                at = a * wide + first + a + 1 + r
                placed[pl.ds(at, 1), :] = chosen[a * reach + r:a * reach + r + 1]
    around = [
        placed[a * wide:a * wide + half, :] + jnp.concatenate(
            [placed[a * wide + half:(a + 1) * wide, :], jnp.zeros((half - reach, lanes), f32)], axis=0
        )
        for a in range(own)
    ]
    fold = lanes // half
    for g in range(0, own, fold):
        group = (around[g:g + fold] * fold)[:fold]
        t = jnp.transpose(jnp.concatenate(group, axis=0))
        for a in range(g, min(g + fold, own)):
            at = (a % fold) * half
            back = (lanes - at) % lanes

            def to_left(re, im):
                re = pltpu.roll(re, back, 1) if back else re
                im = pltpu.roll(im, (back + nvec) % lanes, 1) if (back + nvec) % lanes else im
                return jnp.where(left, jnp.where(real, re, im), 0.0)

            top = around[a] - to_left(t[:half], t[nvec:nvec + half])
            bottom = -to_left(t[half:nvec], t[nvec + half:])
            value = jnp.concatenate([top, bottom], axis=0)
            hi, lo = halves(value)
            low_hi, low_lo = halves(minus_plus * pltpu.roll(value, nvec, 1))
            at = pl.ds(a * lanes, lanes)
            for start in (0, lanes):
                dense_hh[start:start + nvec, at] = hi
                dense_hh[start + nvec:start + lanes, at] = low_hi
            dense_lo[0:nvec, at] = lo
            dense_lo[nvec:lanes, at] = low_lo

    mats_count = combos * 3
    for a in range(0, own, 2):
        at = pl.ds(a * lanes, 2 * lanes)
        got = dot(left_hl[...], dense_hh[:, at]) + dot(left_hl[:, 0:lanes], dense_lo[:, at])
        for b in range(2):
            inner_ref[pl.ds(a + b, mats_count * nvec, stride=own), :] = got[:, b * lanes:(b + 1) * lanes]
    rows = nvec * own
    for m in range(mats_count):
        hi, lo = halves(inner_ref[m * rows:(m + 1) * rows, :])
        inner_hi[m * rows:(m + 1) * rows, :] = hi
        inner_lo[m * rows:(m + 1) * rows, :] = lo
    for r in range(1, chips):
        own_copy(r).wait_recv()
        forward(r).start()
    near_lane = lax.broadcasted_iota(jnp.int32, (rows // 2, lanes), 1) % nvec < half
    for s in range(combos):
        for p in range(3):
            q, r = pairs[p]
            m = s * 3 + p
            at_q = pl.ds((s * 3 + q) * rows, rows)
            at_r = pl.ds((s * 3 + r) * rows, rows)
            left_hi = jnp.concatenate([inner_hi[at_r, :], inner_hi[at_q, :]], axis=1)
            left_lo = jnp.concatenate([inner_lo[at_r, :], inner_lo[at_q, :]], axis=1)
            both = dot(left_hi, right_hl[m])
            whole = both[:, :lanes] + (both[:, lanes:] + dot(left_lo, right_hl[m, :, 0:lanes]))
            up, down = whole[:rows // 2], whole[rows // 2:]
            at = pl.ds(m * (rows // 2), rows // 2)
            cross_w[at, :] = jnp.where(near_lane, down, up)
            same_w[at, :] = -0.5 * jnp.where(near_lane, up, down)

    def at_row(ref, k):
        return jnp.concatenate(
            [ref[(m * half + k) * own:(m * half + k + 1) * own, :] for m in range(mats_count)], axis=0
        )

    c_real = lax.broadcasted_iota(jnp.int32, (count, lanes), 1) < nvec
    for m in range(half // 2):
        even = at_row(same_w, 2 * m)
        odd = at_row(same_w, 2 * m + 1)
        re = jnp.where(c_real, even, pltpu.roll(odd, nvec, 1))
        im = jnp.where(c_real, pltpu.roll(even, nvec, 1), odd)
        at = pl.ds(m * lanes, lanes)
        for start, value in ((0, re), (low, im)):
            hi, lo = halves(value)
            lc_hi[start:start + count, at] = hi
            lc_lo[start:start + count, at] = lo

    own_copy(0).wait_recv()
    for r in range(1, chips):
        forward(r).wait_recv()
    for hf in range(2):
        at = hf * block_rows
        full[at:at + reach * reach, :] = full[at + half * reach:at + block_rows, :]

    inner = lax.broadcasted_iota(jnp.int32, (reach, lanes), 0)
    spot64 = lax.broadcasted_iota(jnp.int32, (nvec, lanes), 1) % nvec
    row64 = lax.broadcasted_iota(jnp.int32, (nvec, lanes), 0)
    crossing = (spot64 >= half) == (row64 < half)
    c_sign = jnp.where(c_real, -1.0, 1.0)
    mid = mid_ref[...]
    turned = pltpu.roll(mid, nvec, 1)
    pad = [jnp.zeros((low - count, nvec), jnp.bfloat16)] if low > count else []
    re_hi, re_lo = halves(mid[:, :nvec])
    im_hi, im_lo = halves(turned[:, :nvec])
    mid_hi = jnp.concatenate([re_hi] + pad + [im_hi], axis=0)
    mid_lo = jnp.concatenate([re_lo] + pad + [im_lo], axis=0)
    mid_k = jnp.concatenate([mid_hi, mid_hi, mid_lo], axis=1)
    one = jnp.zeros((count, lanes), f32)
    two = jnp.zeros((count, lanes), f32)
    for y in range(0, half, 2):
        pair = []
        for k in (y, y + 1):
            parts = []
            for hf in range(2):
                at = hf * block_rows
                before = full[pl.ds(at + reach * k + reach - 1, reach, stride=reach - 1), :]
                behind = full[pl.ds(at + reach * reach + reach * k - 1, reach), :]
                behind = jnp.where(inner == 0, 0.0, -behind)
                slab = jnp.concatenate([before, behind], axis=0)
                shift = (k - reach) % half
                if shift:
                    slab = pltpu.roll(slab, shift, 0)
                slabs[hf * half + k] = slab
                parts.append(slab)
            slab = jnp.concatenate(parts, axis=0)
            hi, lo = halves(slab)
            sl_hl[k * nvec:(k + 1) * nvec, 0:lanes] = hi
            sl_hl[k * nvec:(k + 1) * nvec, lanes:2 * lanes] = lo
            m_hi, m_lo = halves(jnp.where(crossing, slab, 0.0))
            pair.append(jnp.concatenate([m_hi, m_lo, m_hi], axis=0))
        got = dot(mid_k, jnp.concatenate(pair, axis=1))
        for b, k in enumerate((y, y + 1)):
            here = got[:, b * lanes:(b + 1) * lanes]
            value = here[:count] + c_sign * pltpu.roll(here[low:low + count], nvec, 1)
            weight = at_row(cross_w, k)
            one = one + value * weight
            two = two + value * pltpu.roll(weight, nvec, 1)
    both = dot(lc_hi[...], sl_hl[...])
    got = both[:, :lanes] + (both[:, lanes:] + dot(lc_lo[...], sl_hl[:, 0:lanes]))
    value = got[:count] + c_sign * pltpu.roll(got[low:low + count], nvec, 1)
    one = one + value * mid
    two = two + value * turned
    one = jnp.where(c_real, one, -one)
    each = 3 * own
    tile_ref[...] = jnp.concatenate(
        [jnp.sum(one[s * each:(s + 1) * each], axis=0, keepdims=True) for s in range(combos)]
        + [jnp.sum(two[s * each:(s + 1) * each], axis=0, keepdims=True) for s in range(combos)],
        axis=0,
    )

    def sum_copy(r):
        return pltpu.make_async_remote_copy(
            tile_ref, box.at[r - 1], sum_send.at[r - 1], sum_recv.at[r - 1],
            device_id=(tm, (me + r) % n), device_id_type=MESH,
        )

    for r in range(1, n):
        sum_copy(r).start()

    for g in range(half // fold):
        t = jnp.transpose(jnp.concatenate(
            [slabs[other_side * half + g * fold + q] for q in range(fold)], axis=0
        ))
        turn[...] = t
        if own % 8 == 0:
            at = pl.multiple_of(side * half + first, own)
            pick[0, g * own:(g + 1) * own, :] = turn[pl.ds(at, own), :]
            pick[1, g * own:(g + 1) * own, :] = turn[pl.ds(at + nvec, own), :]
        else:
            for r in range(own):
                at = side * half + first + r
                pick[0, g * own + r:g * own + r + 1, :] = turn[pl.ds(at, 1), :]
                pick[1, g * own + r:g * own + r + 1, :] = turn[pl.ds(at + nvec, 1), :]
    steps = half // fold
    quarter = lax.broadcasted_iota(jnp.int32, (steps, lanes), 1) // half
    o_left = lax.broadcasted_iota(jnp.int32, (steps, lanes), 1) % nvec < half

    def shifted(x, by):
        by = by % lanes
        return pltpu.roll(x, by, 1) if by else x

    for g in range(0, own, fold):
        group = [slabs[side * half + first + a] for a in range(g, min(g + fold, own))]
        turn[...] = jnp.transpose(jnp.concatenate((group * fold)[:fold], axis=0))
        at = pl.multiple_of(other_side * half, half)
        re = turn[pl.ds(at, half), :]
        im = turn[pl.ds(at + nvec, half), :]
        turn[0:half, :] = re
        turn[half:2 * half, :] = im
        for a in range(g, min(g + fold, own)):
            for q in range(fold):
                x_re = turn[pl.ds(q, steps, stride=fold), :]
                x_im = turn[pl.ds(half + q, steps, stride=fold), :]
                c_re = pick[0, pl.ds(a, steps, stride=own), :]
                c_im = pick[1, pl.ds(a, steps, stride=own), :]
                back = (a % fold) * half
                value = jnp.where(
                    quarter < 2,
                    jnp.where(quarter == 0, -shifted(x_re, -back), shifted(c_re, half - q * half)),
                    jnp.where(quarter == 2, -shifted(x_im, nvec - back), shifted(c_im, nvec + half - q * half)),
                )
                flipped = jnp.where(o_left, pltpu.roll(value, lanes - half, 1), pltpu.roll(value, half, 1))
                value = jnp.where(side == 1, flipped, value)
                placed[pl.ds(q, steps, stride=fold), :] = value
            board[pl.ds(pl.multiple_of(side * half, half), half), :] = slabs[side * half + first + a]
            board[pl.ds(pl.multiple_of(other_side * half, half), half), :] = placed[0:half, :]
            even, odd = weave(board)
            out_ref[a, pl.ds(0, half, stride=2), :] = even
            out_ref[a, pl.ds(1, half, stride=2), :] = odd

    for s in range(chips):
        pair_copy(s).wait_send()
    for s in range(chips - 1):
        chip_copy(s).wait_send()
    for r in range(1, times):
        tm_copy(r).wait_send()
    own_copy(0).wait_send()
    for r in range(1, chips):
        own_copy(r).wait_send()
        forward(r).wait_send()
    answer = tile_ref[...]
    for r in range(1, n):
        sum_copy(r).wait_recv()
        answer = answer + box[r - 1]
    total = jnp.sum(jnp.transpose(answer), axis=0, keepdims=True) * corr_scale
    corr_ref[...] = jnp.concatenate([total[:, :combos], total[:, combos:]], axis=0)
    for r in range(1, n):
        sum_copy(r).wait_send()


def shards(vectors, perambulators, shift_steps, spin_choice):
    vec = vectors[0]
    _, _, nvec, sites = vec.shape
    spin_pairs = perambulators.shape[1]
    combos = spin_choice.shape[0]
    n = lax.axis_size("space")
    times = lax.axis_size("tm")
    own, half, lanes = nvec // n, nvec // 2, 2 * nvec
    reach = half // 2
    wide = half + reach
    share = own * reach
    chips = n // 2
    count = combos * 3 * own
    low = -(-count // 16) * 16
    scale = 1.0 / math.sqrt(24.0 * sites * n)
    corr_scale = 0.25 / (nvec * math.sqrt(nvec))
    mats = perambulators[0].reshape(spin_pairs, 2, half, lanes)
    mats = jnp.transpose(mats, (0, 2, 1, 3)).reshape(spin_pairs, nvec, lanes)
    tile = (share, lanes)
    f32, bf16 = jnp.float32, jnp.bfloat16
    dma = pltpu.SemaphoreType.DMA
    smem = pl.BlockSpec(memory_space=pltpu.SMEM)
    anywhere = pl.BlockSpec(memory_space=pl.ANY)
    out, correlator = pl.pallas_call(
        functools.partial(elementals_kernel, n, times, scale, corr_scale),
        out_shape=(
            pltpu.VMEM((own, nvec, lanes), f32),
            pltpu.VMEM((2, combos), f32),
        ),
        in_specs=[anywhere, anywhere, anywhere, smem],
        out_specs=(VM, VM),
        scratch_shapes=[
            pltpu.VMEM(vec.shape, f32),
            pltpu.VMEM(mats.shape, f32),
            pltpu.SMEM(shift_steps.shape, jnp.int32),
            dma((8,)),
            pltpu.VMEM((2, 3, sites // 128, 4 * wide, 128), f32),
            pltpu.VMEM((4 * nvec, 6 * sites), bf16),
            pltpu.VMEM((2, 2 * share, 6 * sites), bf16),
            pltpu.VMEM((2, 2 * share, 6 * sites), bf16),
            pltpu.VMEM((chips,) + tile, f32),
            pltpu.VMEM((chips,) + tile, f32),
            pltpu.VMEM((chips,) + tile, f32),
            pltpu.VMEM((chips - 1,) + tile, f32),
            pltpu.VMEM(tile, f32),
            pltpu.VMEM((2 * wide * reach, lanes), f32),
            pltpu.VMEM((times - 1,) + tile, f32),
            pltpu.VMEM((nvec, lanes), f32),
            pltpu.VMEM((combos, 3, nvec, lanes), f32),
            pltpu.VMEM((combos, 3, nvec, lanes), f32),
            pltpu.VMEM((combos * 3, 2 * lanes, 2 * lanes), bf16),
            pltpu.VMEM((combos * 3 * nvec, 2 * lanes), bf16),
            pltpu.VMEM((max(own, 2) * wide, lanes), f32),
            pltpu.VMEM((2 * lanes, own * lanes), bf16),
            pltpu.VMEM((lanes, own * lanes), bf16),
            pltpu.VMEM((combos * 3 * nvec * own, lanes), f32),
            pltpu.VMEM((combos * 3 * nvec * own, lanes), bf16),
            pltpu.VMEM((combos * 3 * nvec * own, lanes), bf16),
            pltpu.VMEM((count * half, lanes), f32),
            pltpu.VMEM((count * half, lanes), f32),
            pltpu.VMEM((2 * low, half * nvec), bf16),
            pltpu.VMEM((2 * low, half * nvec), bf16),
            pltpu.VMEM((count, lanes), f32),
            pltpu.VMEM((nvec, half, lanes), f32),
            pltpu.VMEM((half * nvec, 2 * lanes), bf16),
            pltpu.VMEM((lanes, lanes), f32),
            pltpu.VMEM((2, own * (nvec // 8), lanes), f32),
            pltpu.VMEM((2 * combos, lanes), f32),
            pltpu.VMEM((n - 1, 2 * combos, lanes), f32),
            dma((chips,)), dma((chips,)),
            dma((chips - 1,)), dma((chips - 1,)),
            dma((chips,)), dma((chips,)),
            dma((chips - 1,)), dma((chips - 1,)),
            dma((times - 1,)), dma((times - 1,)),
            dma((n - 1,)), dma((n - 1,)),
        ],
        compiler_params=pltpu.CompilerParams(
            collective_id=0, has_side_effects=True, vmem_limit_bytes=60 * 1024 * 1024
        ),
        name="elementals",
    )(vec, mats, shift_steps, spin_choice)
    out = jnp.transpose(out.reshape(own, half, 2, lanes), (0, 2, 1, 3))
    return (out.reshape(1, own, 2, nvec * nvec), jnp.transpose(correlator)[None])


def solution(mesh):
    placed = (P("tm", None, None, None, "space"), P("tm", None, None, None), P("tm"), P())
    return jax.shard_map(
        shards,
        mesh=mesh,
        in_specs=placed,
        out_specs=(P("tm", "space", None, None), P("tm", None, None)),
        check_vma=False,
    )
```

```python
import functools
import math

import jax
import jax.numpy as jnp
from jax import lax
from jax.experimental import pallas as pl
from jax.experimental.pallas import tpu as pltpu
from jax.sharding import PartitionSpec as P

MESH = pl.DeviceIdType.MESH
VM = pl.BlockSpec(memory_space=pltpu.VMEM)
NT_DIMS = (((1,), (1,)), ((), ()))


def halves(x):
    top = x.astype(jnp.bfloat16)
    return top, (x - top.astype(jnp.float32)).astype(jnp.bfloat16)


def dot(a, b):
    return jnp.dot(a, b, preferred_element_type=jnp.float32)


def elementals_kernel(
    n, times, scale, corr_scale, v_hbm, mats_hbm, shift_hbm, spin_ref, out_ref, corr_ref,
    v_ref, mats_ref, shift_ref, in_sem, vv, lead, d_hi, d_lo, keep, give, pair_in, chip_in, own_ref, full, sink_ref,
    board, spin_mats, local_mats, right_hl, left_hl, placed, dense_hh, dense_lo,
    inner_ref, cross_w, same_w, lc_hi, lc_lo, mid_ref, slabs, sl_hl,
    turn, pick, tile_ref, box,
    pair_send, pair_recv, chip_send, chip_recv,
    own_send, own_recv, fwd_send, fwd_recv, tm_send, tm_recv,
    sum_send, sum_recv, through_in, through_send, through_recv,
):
    f32 = jnp.float32
    me = lax.axis_index("space")
    tm = lax.axis_index("tm")
    chips = n // 2
    chip = me // 2
    core = me % 2
    mate = chip * 2 + 1 - core
    nvec = v_ref.shape[2]
    sites = v_ref.shape[3]
    own = nvec // n
    half = nvec // 2
    lanes = 2 * nvec
    reach = half // 2
    share = own * reach
    per_half = n // 2
    wide = half + reach
    block_rows = wide * reach
    side = me // per_half
    other_side = 1 - side
    first = (me % per_half) * own
    combos = spin_ref.shape[0]
    count = combos * 3 * own
    low = -(-count // 16) * 16

    def partner(m, back=False):
        if chips & (chips - 1):
            return (chip + chips - m) % chips if back else (chip + m) % chips
        out, bit = 0, 1
        while bit < chips:
            mine, its = chip // bit % 2, m // bit % 2
            out = out + bit * (mine + its - 2 * mine * its)
            bit *= 2
        return out

    barrier = pltpu.get_barrier_semaphore()
    for r in range(1, n):
        pl.semaphore_signal(barrier, inc=1, device_id=(tm, (me + r) % n), device_id_type=MESH)
    for r in range(1, times):
        pl.semaphore_signal(
            barrier, inc=1, device_id=((tm + r) % times, me), device_id_type=MESH
        )

    vec_loads = [
        [
            pltpu.make_async_copy(v_hbm.at[c, a], v_ref.at[c, a], in_sem.at[c * 3 + a])
            for a in range(3)
        ]
        for c in range(2)
    ]
    mat_load = pltpu.make_async_copy(mats_hbm, mats_ref, in_sem.at[6])
    shift_load = pltpu.make_async_copy(shift_hbm, shift_ref, in_sem.at[7])
    for a in range(3):
        vec_loads[0][a].start()
        vec_loads[1][a].start()

    for a in range(3):
        vec_loads[0][a].wait()
        vec_loads[1][a].wait()
        re = v_ref[0, a]
        im = v_ref[1, a]
        re_hi, re_lo = halves(re)
        im_hi, im_lo = halves(im)
        one = pl.ds(a * sites, sites)
        two = pl.ds((3 + a) * sites, sites)
        lead[0:nvec, one] = re_hi
        lead[0:nvec, two] = -im_hi
        lead[nvec:lanes, one] = im_hi
        lead[nvec:lanes, two] = re_hi
        lead[lanes:lanes + nvec, one] = re_lo
        lead[lanes:lanes + nvec, two] = -im_lo
        lead[lanes + nvec:2 * lanes, one] = im_lo
        lead[lanes + nvec:2 * lanes, two] = re_lo
        for c, value in enumerate((re, im)):
            for hf in range(2):
                part = value[hf * half:(hf + 1) * half]
                for b in range(sites // 128):
                    cut = part[:, b * 128:(b + 1) * 128]
                    vv[c, a, b, pl.ds(2 * hf * wide, half, stride=2), :] = cut
                    vv[c, a, b, pl.ds(2 * (hf * wide + half), reach, stride=2), :] = cut[:reach]

    mat_load.start()
    shift_load.start()

    def fill(dest, slot, buf):
        base = (dest // per_half) * wide + (dest % per_half) * own
        for a in range(own):
            at = pl.ds(slot * share + a * reach, reach)
            for cut in range(sites // 128):
                mine = [[vv[c, x, cut, pl.ds(2 * (base + a), 1), :] for x in range(3)] for c in range(2)]
                other = [
                    [vv[c, x, cut, pl.ds(2 * (base + a + 1), reach, stride=2), :] for x in range(3)]
                    for c in range(2)
                ]
                for m in range(3):
                    b, d = (m + 1) % 3, (m + 2) % 3
                    real_part = (
                        mine[0][b] * other[0][d] - mine[1][b] * other[1][d]
                        - (mine[0][d] * other[0][b] - mine[1][d] * other[1][b])
                    )
                    imag_part = (
                        mine[0][b] * other[1][d] + mine[1][b] * other[0][d]
                        - (mine[0][d] * other[1][b] + mine[1][d] * other[0][b])
                    )
                    for q, value in ((m, real_part), (3 + m, imag_part)):
                        hi, lo = halves(value)
                        where = q * sites + cut * 128
                        d_hi[buf, at, where:where + 128] = hi
                        d_lo[buf, at, where:where + 128] = lo

    def pair_copy(s):
        return pltpu.make_async_remote_copy(
            give.at[s], pair_in.at[s], pair_send.at[s], pair_recv.at[s],
            device_id=(tm, mate), device_id_type=MESH,
        )

    def chip_copy(s):
        return pltpu.make_async_remote_copy(
            keep.at[s], chip_in.at[s], chip_send.at[s], chip_recv.at[s],
            device_id=(tm, partner(chips - 1 - s) * 2 + core), device_id_type=MESH,
        )

    def fills(group, buf):
        for slot, (part, s) in enumerate(group):
            fill(partner(chips - 1 - s) * 2 + (1 - core if part == 0 else core), slot, buf)

    def products(group, buf):
        at = pl.ds(0, len(group) * share)
        both = lax.dot_general(d_hi[buf, at, :], lead[...], NT_DIMS, preferred_element_type=f32)
        rest = lax.dot_general(d_lo[buf, at, :], lead[0:lanes], NT_DIMS, preferred_element_type=f32)
        got = both[:, :lanes] + (both[:, lanes:] + rest)
        for slot, (part, s) in enumerate(group):
            (give, keep)[part][s] = got[slot * share:(slot + 1) * share]

    def add_pair(s):
        pair_copy(s).wait_recv()
        keep[s] = keep[s] + pair_in[s]

    outer = chip % 3 == 0
    through = pltpu.make_async_remote_copy(
        keep.at[0], through_in, through_send, through_recv,
        device_id=(tm, partner(1) * 2 + core), device_id_type=MESH,
    )

    def relay(s):
        pair_copy(s).wait_recv()
        keep[s] = keep[s] + pair_in[s]
        chip_copy(s).start()

    def one_chip(s, carry):
        for part in range(2):
            fill(partner(chips - 1 - s) * 2 + (1 - core if part == 0 else core), part, 0)
        both = lax.dot_general(d_hi[0], lead[...], NT_DIMS, preferred_element_type=f32)
        rest = lax.dot_general(d_lo[0], lead[0:lanes], NT_DIMS, preferred_element_type=f32)
        got = both[:, :lanes] + (both[:, lanes:] + rest)
        give[s] = got[:share]
        keep[s] = got[share:]
        pair_copy(s).start()

        @pl.when(s > 0)
        def _():
            relay(s - 1)

        return carry

    if chips == 4:
        groups = (((0, 0),), ((0, 1), (0, 2)), ((1, 0), (0, 3)), ((1, 1), (1, 2)), ((1, 3),))
        fills(groups[0], 0)
        for k, group in enumerate(groups):
            products(group, k % 2)
            if k + 1 < len(groups):
                fills(groups[k + 1], (k + 1) % 2)
            if k == 0:
                pl.semaphore_wait(barrier, n - 1 + times - 1)
            for part, s in group:
                if part == 0:
                    pair_copy(s).start()
            if k == 2:
                add_pair(0)
                pl.when(outer)(through.start)
                pl.when(jnp.logical_not(outer))(chip_copy(0).start)
        add_pair(1)
        pl.when(outer)(chip_copy(1).start)
        relay(2)

        @pl.when(jnp.logical_not(outer))
        def _():
            through.wait_recv()
            keep[1] = keep[1] + through_in[...]
            chip_copy(1).start()

    else:
        pl.semaphore_wait(barrier, n - 1 + times - 1)
        lax.fori_loop(0, chips, one_chip, 0)

    lane = lax.broadcasted_iota(jnp.int32, (half, lanes), 1)
    spot = lane % nvec
    left = spot < half
    real = lane < nvec
    minus_plus = jnp.where(lax.broadcasted_iota(jnp.int32, (nvec, lanes), 1) < nvec, -1.0, 1.0)

    def weave(ref):
        even = ref[pl.ds(0, half, stride=2), :]
        odd = ref[pl.ds(1, half, stride=2), :]
        return (
            jnp.where(real, even, pltpu.roll(odd, nvec, 1)),
            jnp.where(real, pltpu.roll(even, nvec, 1), odd),
        )

    pairs = ((1, 2), (0, 2), (0, 1))
    mat_load.wait()
    shift_load.wait()
    for s in range(combos):
        for q in range(3):
            board[...] = mats_ref[spin_ref[s, q]]
            even, odd = weave(board)
            spin_mats[s, q, pl.ds(0, half, stride=2), :] = even
            spin_mats[s, q, pl.ds(1, half, stride=2), :] = odd
            near = spin_mats[s, q, pl.ds(pl.multiple_of(side * half, half), half), :]
            far = spin_mats[s, q, pl.ds(pl.multiple_of(other_side * half, half), half), :]
            local = jnp.concatenate([near, far], axis=0)
            local_mats[s, q] = local
            parts = halves(local) + halves(minus_plus * pltpu.roll(local, nvec, 1))
            for p in range(3):
                if q in pairs[p]:
                    at = pairs[p].index(q) * lanes
                    for row, top, low_part in ((0, parts[0], parts[2]), (lanes, parts[1], parts[3])):
                        right_hl[s * 3 + p, at:at + nvec, row:row + lanes] = top
                        right_hl[s * 3 + p, at + nvec:at + lanes, row:row + lanes] = low_part
    flat = [(s, q) for s in range(combos) for q in range(3)]
    wide_real = lax.broadcasted_iota(jnp.int32, (nvec, lanes), 1) < nvec
    for m in range(0, len(flat), 2):
        ahead = flat[m + 1] if m + 1 < len(flat) else flat[m]
        t = jnp.transpose(jnp.concatenate([local_mats[flat[m]], local_mats[ahead]], axis=0))
        up, down = t[:nvec], t[nvec:]
        here = jnp.where(wide_real, up, pltpu.roll(down, nvec, 1))
        there = jnp.where(wide_real, pltpu.roll(up, nvec, 1), down)
        for k, value in ((m, here), (m + 1, there)):
            if k < len(flat):
                hi, lo = halves(value)
                left_hl[k * nvec:(k + 1) * nvec, 0:lanes] = hi
                left_hl[k * nvec:(k + 1) * nvec, lanes:2 * lanes] = lo
    for s in range(combos):
        for p in range(3):
            if own % 8 == 0:
                rows = spin_mats[s, p, pl.ds(pl.multiple_of(me * own, own), own), :]
                mid_ref[(s * 3 + p) * own:(s * 3 + p + 1) * own, :] = rows
            else:
                for r in range(own):
                    at = (s * 3 + p) * own + r
                    mid_ref[at:at + 1, :] = spin_mats[s, p, pl.ds(me * own + r, 1), :]

    last = chips - 1
    pair_copy(last).wait_recv()
    total = keep[last] + pair_in[last]
    if chips == 4:
        for s in (1, 2):
            chip_copy(s).wait_recv()
            total = total + chip_in[s]
        own_ref[...] = total * scale

        @pl.when(jnp.logical_not(outer))
        def _():
            chip_copy(0).wait_recv()
            own_ref[...] = (total + chip_in[0]) * scale
    else:
        for s in range(last):
            chip_copy(s).wait_recv()
            total = total + chip_in[s]
        own_ref[...] = total * scale

    def rows_of(d):
        start = (d // per_half) * block_rows + reach * reach + (d % per_half) * share
        return pl.ds(pl.multiple_of(start, reach), share)

    def tm_copy(r):
        return pltpu.make_async_remote_copy(
            own_ref, sink_ref.at[r - 1], tm_send.at[r - 1], tm_recv.at[r - 1],
            device_id=((tm + r) % times, me), device_id_type=MESH,
        )

    def own_copy(r):
        target = mate if r == 0 else partner(r) * 2 + core
        return pltpu.make_async_remote_copy(
            own_ref, full.at[rows_of(me)], own_send.at[r], own_recv.at[r],
            device_id=(tm, target), device_id_type=MESH,
        )

    def forward(r):
        at = rows_of(partner(r, True) * 2 + core)
        return pltpu.make_async_remote_copy(
            full.at[at], full.at[at], fwd_send.at[r - 1], fwd_recv.at[r - 1],
            device_id=(tm, mate), device_id_type=MESH,
        )

    for r in range(1, times):
        tm_copy(r).start()
    for r in range(chips - 1, 0, -1):
        own_copy(r).start()
    own_copy(0).start()
    full[rows_of(me), :] = own_ref[...]

    for r in range(1, times):
        tm_copy(r).wait_recv()
    chosen = sink_ref[jnp.clip(times - 1 - shift_ref[0], 0, times - 2)]
    wide_lane = lax.broadcasted_iota(jnp.int32, (share, lanes), 1)
    wide_left = wide_lane % nvec < half
    swapped = jnp.where(wide_left, pltpu.roll(chosen, lanes - half, 1), pltpu.roll(chosen, half, 1))
    chosen = jnp.where(side == 1, swapped, chosen)
    step_of = lax.broadcasted_iota(jnp.int32, (share, lanes), 0) % reach
    factor = jnp.where(wide_left, 1.0 / 3.0, 1.0) * jnp.where(step_of == reach - 1, 0.5, 1.0)
    chosen = chosen * jnp.where(wide_lane < nvec, factor, -factor)
    placed[...] = jnp.zeros_like(placed)
    for a in range(own):
        if own % 8 == 0:
            start = pl.multiple_of(a * wide + first, 8)
            view = placed.at[pl.ds(start, own + reach), :]
            view[a + 1:a + 1 + reach, :] = chosen[a * reach:(a + 1) * reach]
        else:
            for r in range(reach):
                at = a * wide + first + a + 1 + r
                placed[pl.ds(at, 1), :] = chosen[a * reach + r:a * reach + r + 1]
    around = [
        placed[a * wide:a * wide + half, :] + jnp.concatenate(
            [placed[a * wide + half:(a + 1) * wide, :], jnp.zeros((half - reach, lanes), f32)], axis=0
        )
        for a in range(own)
    ]
    fold = lanes // half
    for g in range(0, own, fold):
        group = (around[g:g + fold] * fold)[:fold]
        t = jnp.transpose(jnp.concatenate(group, axis=0))
        for a in range(g, min(g + fold, own)):
            at = (a % fold) * half
            back = (lanes - at) % lanes

            def to_left(re, im):
                re = pltpu.roll(re, back, 1) if back else re
                im = pltpu.roll(im, (back + nvec) % lanes, 1) if (back + nvec) % lanes else im
                return jnp.where(left, jnp.where(real, re, im), 0.0)

            top = around[a] - to_left(t[:half], t[nvec:nvec + half])
            bottom = -to_left(t[half:nvec], t[nvec + half:])
            value = jnp.concatenate([top, bottom], axis=0)
            hi, lo = halves(value)
            low_hi, low_lo = halves(minus_plus * pltpu.roll(value, nvec, 1))
            at = pl.ds(a * lanes, lanes)
            for start in (0, lanes):
                dense_hh[start:start + nvec, at] = hi
                dense_hh[start + nvec:start + lanes, at] = low_hi
            dense_lo[0:nvec, at] = lo
            dense_lo[nvec:lanes, at] = low_lo

    mats_count = combos * 3
    for a in range(0, own, 2):
        at = pl.ds(a * lanes, 2 * lanes)
        got = dot(left_hl[...], dense_hh[:, at]) + dot(left_hl[:, 0:lanes], dense_lo[:, at])
        for b in range(2):
            inner_ref[pl.ds(a + b, mats_count * nvec, stride=own), :] = got[:, b * lanes:(b + 1) * lanes]
    rows = nvec * own
    for r in range(1, chips):
        own_copy(r).wait_recv()
        forward(r).start()
    near_lane = lax.broadcasted_iota(jnp.int32, (rows // 2, lanes), 1) % nvec < half
    for s in range(combos):
        for p in range(3):
            q, r = pairs[p]
            m = s * 3 + p
            at_q = pl.ds((s * 3 + q) * rows, rows)
            at_r = pl.ds((s * 3 + r) * rows, rows)
            left_hi, left_lo = halves(jnp.concatenate([inner_ref[at_r, :], inner_ref[at_q, :]], axis=1))
            both = dot(left_hi, right_hl[m])
            whole = both[:, :lanes] + (both[:, lanes:] + dot(left_lo, right_hl[m, :, 0:lanes]))
            up, down = whole[:rows // 2], whole[rows // 2:]
            at = pl.ds(m * (rows // 2), rows // 2)
            cross_w[at, :] = jnp.where(near_lane, down, up)
            same_w[at, :] = -0.5 * jnp.where(near_lane, up, down)

    def at_row(ref, k):
        return jnp.concatenate(
            [ref[(m * half + k) * own:(m * half + k + 1) * own, :] for m in range(mats_count)], axis=0
        )

    c_real = lax.broadcasted_iota(jnp.int32, (count, lanes), 1) < nvec
    for m in range(half // 2):
        even = at_row(same_w, 2 * m)
        odd = at_row(same_w, 2 * m + 1)
        re = jnp.where(c_real, even, pltpu.roll(odd, nvec, 1))
        im = jnp.where(c_real, pltpu.roll(even, nvec, 1), odd)
        at = pl.ds(m * lanes, lanes)
        for start, value in ((0, re), (low, im)):
            hi, lo = halves(value)
            lc_hi[start:start + count, at] = hi
            lc_lo[start:start + count, at] = lo

    own_copy(0).wait_recv()
    for r in range(1, chips):
        forward(r).wait_recv()
    for hf in range(2):
        at = hf * block_rows
        full[at:at + reach * reach, :] = full[at + half * reach:at + block_rows, :]

    inner = lax.broadcasted_iota(jnp.int32, (reach, lanes), 0)
    spot64 = lax.broadcasted_iota(jnp.int32, (nvec, lanes), 1) % nvec
    row64 = lax.broadcasted_iota(jnp.int32, (nvec, lanes), 0)
    crossing = (spot64 >= half) == (row64 < half)
    c_sign = jnp.where(c_real, -1.0, 1.0)
    mid = mid_ref[...]
    turned = pltpu.roll(mid, nvec, 1)
    pad = [jnp.zeros((low - count, nvec), jnp.bfloat16)] if low > count else []
    re_hi, re_lo = halves(mid[:, :nvec])
    im_hi, im_lo = halves(turned[:, :nvec])
    mid_hi = jnp.concatenate([re_hi] + pad + [im_hi], axis=0)
    mid_lo = jnp.concatenate([re_lo] + pad + [im_lo], axis=0)
    mid_k = jnp.concatenate([mid_hi, mid_hi, mid_lo], axis=1)
    one = jnp.zeros((count, lanes), f32)
    two = jnp.zeros((count, lanes), f32)
    got_same = None
    for y in range(0, half, 2):
        pair = []
        for k in (y, y + 1):
            parts = []
            for hf in range(2):
                at = hf * block_rows
                before = full[pl.ds(at + reach * k + reach - 1, reach, stride=reach - 1), :]
                behind = full[pl.ds(at + reach * reach + reach * k - 1, reach), :]
                behind = jnp.where(inner == 0, 0.0, -behind)
                slab = jnp.concatenate([before, behind], axis=0)
                shift = (k - reach) % half
                if shift:
                    slab = pltpu.roll(slab, shift, 0)
                slabs[hf * half + k] = slab
                parts.append(slab)
            slab = jnp.concatenate(parts, axis=0)
            hi, lo = halves(slab)
            sl_hl[k * nvec:(k + 1) * nvec, 0:lanes] = hi
            sl_hl[k * nvec:(k + 1) * nvec, lanes:2 * lanes] = lo
            m_hi, m_lo = halves(jnp.where(crossing, slab, 0.0))
            pair.append(jnp.concatenate([m_hi, m_lo, m_hi], axis=0))
        got = dot(mid_k, jnp.concatenate(pair, axis=1))
        for b, k in enumerate((y, y + 1)):
            here = got[:, b * lanes:(b + 1) * lanes]
            value = here[:count] + c_sign * pltpu.roll(here[low:low + count], nvec, 1)
            weight = at_row(cross_w, k)
            one = one + value * weight
            two = two + value * pltpu.roll(weight, nvec, 1)
        if (y + 2) % (half // 4) == 0:
            at = pl.ds((y + 2 - half // 4) * nvec, half // 4 * nvec)
            both = dot(lc_hi[:, at], sl_hl[at, :])
            both = both[:, :lanes] + (both[:, lanes:] + dot(lc_lo[:, at], sl_hl[at, 0:lanes]))
            got_same = both if got_same is None else got_same + both
    got = got_same
    value = got[:count] + c_sign * pltpu.roll(got[low:low + count], nvec, 1)
    one = one + value * mid
    two = two + value * turned
    one = jnp.where(c_real, one, -one)
    each = 3 * own
    tile_ref[...] = jnp.concatenate(
        [jnp.sum(one[s * each:(s + 1) * each], axis=0, keepdims=True) for s in range(combos)]
        + [jnp.sum(two[s * each:(s + 1) * each], axis=0, keepdims=True) for s in range(combos)],
        axis=0,
    )

    def sum_copy(r):
        return pltpu.make_async_remote_copy(
            tile_ref, box.at[r - 1], sum_send.at[r - 1], sum_recv.at[r - 1],
            device_id=(tm, (me + r) % n), device_id_type=MESH,
        )

    for r in range(1, n):
        sum_copy(r).start()

    for g in range(half // fold):
        t = jnp.transpose(jnp.concatenate(
            [slabs[other_side * half + g * fold + q] for q in range(fold)], axis=0
        ))
        turn[...] = t
        if own % 8 == 0:
            at = pl.multiple_of(side * half + first, own)
            pick[0, g * own:(g + 1) * own, :] = turn[pl.ds(at, own), :]
            pick[1, g * own:(g + 1) * own, :] = turn[pl.ds(at + nvec, own), :]
        else:
            for r in range(own):
                at = side * half + first + r
                pick[0, g * own + r:g * own + r + 1, :] = turn[pl.ds(at, 1), :]
                pick[1, g * own + r:g * own + r + 1, :] = turn[pl.ds(at + nvec, 1), :]
    steps = half // fold
    quarter = lax.broadcasted_iota(jnp.int32, (steps, lanes), 1) // half
    o_left = lax.broadcasted_iota(jnp.int32, (steps, lanes), 1) % nvec < half

    def shifted(x, by):
        by = by % lanes
        return pltpu.roll(x, by, 1) if by else x

    for g in range(0, own, fold):
        group = [slabs[side * half + first + a] for a in range(g, min(g + fold, own))]
        turn[...] = jnp.transpose(jnp.concatenate((group * fold)[:fold], axis=0))
        at = pl.multiple_of(other_side * half, half)
        re = turn[pl.ds(at, half), :]
        im = turn[pl.ds(at + nvec, half), :]
        turn[0:half, :] = re
        turn[half:2 * half, :] = im
        for a in range(g, min(g + fold, own)):
            for q in range(fold):
                x_re = turn[pl.ds(q, steps, stride=fold), :]
                x_im = turn[pl.ds(half + q, steps, stride=fold), :]
                c_re = pick[0, pl.ds(a, steps, stride=own), :]
                c_im = pick[1, pl.ds(a, steps, stride=own), :]
                back = (a % fold) * half
                value = jnp.where(
                    quarter < 2,
                    jnp.where(quarter == 0, -shifted(x_re, -back), shifted(c_re, half - q * half)),
                    jnp.where(quarter == 2, -shifted(x_im, nvec - back), shifted(c_im, nvec + half - q * half)),
                )
                flipped = jnp.where(o_left, pltpu.roll(value, lanes - half, 1), pltpu.roll(value, half, 1))
                value = jnp.where(side == 1, flipped, value)
                placed[pl.ds(q, steps, stride=fold), :] = value
            board[pl.ds(pl.multiple_of(side * half, half), half), :] = slabs[side * half + first + a]
            board[pl.ds(pl.multiple_of(other_side * half, half), half), :] = placed[0:half, :]
            even, odd = weave(board)
            out_ref[a, pl.ds(0, half, stride=2), :] = even
            out_ref[a, pl.ds(1, half, stride=2), :] = odd

    for s in range(chips):
        pair_copy(s).wait_send()
    if chips == 4:
        pl.when(outer)(through.wait_send)
        pl.when(jnp.logical_not(outer))(chip_copy(0).wait_send)
        chip_copy(1).wait_send()
        chip_copy(2).wait_send()
    else:
        for s in range(chips - 1):
            chip_copy(s).wait_send()
    for r in range(1, times):
        tm_copy(r).wait_send()
    own_copy(0).wait_send()
    for r in range(1, chips):
        own_copy(r).wait_send()
        forward(r).wait_send()
    answer = tile_ref[...]
    for r in range(1, n):
        sum_copy(r).wait_recv()
        answer = answer + box[r - 1]
    total = jnp.sum(jnp.transpose(answer), axis=0, keepdims=True) * corr_scale
    corr_ref[...] = jnp.concatenate([total[:, :combos], total[:, combos:]], axis=0)
    for r in range(1, n):
        sum_copy(r).wait_send()


def shards(vectors, perambulators, shift_steps, spin_choice):
    vec = vectors[0]
    _, _, nvec, sites = vec.shape
    spin_pairs = perambulators.shape[1]
    combos = spin_choice.shape[0]
    n = lax.axis_size("space")
    times = lax.axis_size("tm")
    own, half, lanes = nvec // n, nvec // 2, 2 * nvec
    reach = half // 2
    wide = half + reach
    share = own * reach
    chips = n // 2
    count = combos * 3 * own
    low = -(-count // 16) * 16
    scale = 1.0 / math.sqrt(24.0 * sites * n)
    corr_scale = 0.25 / (nvec * math.sqrt(nvec))
    mats = perambulators[0].reshape(spin_pairs, 2, half, lanes)
    mats = jnp.transpose(mats, (0, 2, 1, 3)).reshape(spin_pairs, nvec, lanes)
    tile = (share, lanes)
    f32, bf16 = jnp.float32, jnp.bfloat16
    dma = pltpu.SemaphoreType.DMA
    smem = pl.BlockSpec(memory_space=pltpu.SMEM)
    anywhere = pl.BlockSpec(memory_space=pl.ANY)
    out, correlator = pl.pallas_call(
        functools.partial(elementals_kernel, n, times, scale, corr_scale),
        out_shape=(
            pltpu.VMEM((own, nvec, lanes), f32),
            pltpu.VMEM((2, combos), f32),
        ),
        in_specs=[anywhere, anywhere, anywhere, smem],
        out_specs=(VM, VM),
        scratch_shapes=[
            pltpu.VMEM(vec.shape, f32),
            pltpu.VMEM(mats.shape, f32),
            pltpu.SMEM(shift_steps.shape, jnp.int32),
            dma((8,)),
            pltpu.VMEM((2, 3, sites // 128, 4 * wide, 128), f32),
            pltpu.VMEM((4 * nvec, 6 * sites), bf16),
            pltpu.VMEM((2, 2 * share, 6 * sites), bf16),
            pltpu.VMEM((2, 2 * share, 6 * sites), bf16),
            pltpu.VMEM((chips,) + tile, f32),
            pltpu.VMEM((chips,) + tile, f32),
            pltpu.VMEM((chips,) + tile, f32),
            pltpu.VMEM((chips - 1,) + tile, f32),
            pltpu.VMEM(tile, f32),
            pltpu.VMEM((2 * wide * reach, lanes), f32),
            pltpu.VMEM((times - 1,) + tile, f32),
            pltpu.VMEM((nvec, lanes), f32),
            pltpu.VMEM((combos, 3, nvec, lanes), f32),
            pltpu.VMEM((combos, 3, nvec, lanes), f32),
            pltpu.VMEM((combos * 3, 2 * lanes, 2 * lanes), bf16),
            pltpu.VMEM((combos * 3 * nvec, 2 * lanes), bf16),
            pltpu.VMEM((max(own, 2) * wide, lanes), f32),
            pltpu.VMEM((2 * lanes, own * lanes), bf16),
            pltpu.VMEM((lanes, own * lanes), bf16),
            pltpu.VMEM((combos * 3 * nvec * own, lanes), f32),
            pltpu.VMEM((count * half, lanes), f32),
            pltpu.VMEM((count * half, lanes), f32),
            pltpu.VMEM((2 * low, half * nvec), bf16),
            pltpu.VMEM((2 * low, half * nvec), bf16),
            pltpu.VMEM((count, lanes), f32),
            pltpu.VMEM((nvec, half, lanes), f32),
            pltpu.VMEM((half * nvec, 2 * lanes), bf16),
            pltpu.VMEM((lanes, lanes), f32),
            pltpu.VMEM((2, own * (nvec // 8), lanes), f32),
            pltpu.VMEM((2 * combos, lanes), f32),
            pltpu.VMEM((n - 1, 2 * combos, lanes), f32),
            dma((chips,)), dma((chips,)),
            dma((chips - 1,)), dma((chips - 1,)),
            dma((chips,)), dma((chips,)),
            dma((chips - 1,)), dma((chips - 1,)),
            dma((times - 1,)), dma((times - 1,)),
            dma((n - 1,)), dma((n - 1,)),
            pltpu.VMEM(tile, f32), dma, dma,
        ],
        compiler_params=pltpu.CompilerParams(
            collective_id=0, has_side_effects=True, vmem_limit_bytes=60 * 1024 * 1024
        ),
        name="elementals",
    )(vec, mats, shift_steps, spin_choice)
    out = jnp.transpose(out.reshape(own, half, 2, lanes), (0, 2, 1, 3))
    return (out.reshape(1, own, 2, nvec * nvec), jnp.transpose(correlator)[None])


def solution(mesh):
    placed = (P("tm", None, None, None, "space"), P("tm", None, None, None), P("tm"), P())
    return jax.shard_map(
        shards,
        mesh=mesh,
        in_specs=placed,
        out_specs=(P("tm", "space", None, None), P("tm", None, None)),
        check_vma=False,
    )
```

```python
import functools
import math

import jax
import jax.numpy as jnp
from jax import lax
from jax.experimental import pallas as pl
from jax.experimental.pallas import tpu as pltpu
from jax.sharding import PartitionSpec as P

MESH = pl.DeviceIdType.MESH
VM = pl.BlockSpec(memory_space=pltpu.VMEM)
NT_DIMS = (((1,), (1,)), ((), ()))


def halves(x):
    top = x.astype(jnp.bfloat16)
    return top, (x - top.astype(jnp.float32)).astype(jnp.bfloat16)


def dot(a, b):
    return jnp.dot(a, b, preferred_element_type=jnp.float32)


def elementals_kernel(
    n, times, scale, corr_scale, v_hbm, mats_hbm, shift_hbm, spin_ref, out_ref, corr_ref,
    v_ref, mats_ref, shift_ref, in_sem, vv, lead, d_hi, d_lo, keep, give, pair_in, chip_in, own_ref, full, sink_ref,
    board, spin_mats, local_mats, right_hl, left_hl, placed, dense_hh, dense_lo,
    inner_ref, cross_w, same_w, lc_hi, lc_lo, mid_ref, slabs, sl_hl,
    turn, pick, tile_ref, box,
    pair_send, pair_recv, chip_send, chip_recv,
    own_send, own_recv, fwd_send, fwd_recv, tm_send, tm_recv,
    sum_send, sum_recv, through_in, through_send, through_recv,
):
    f32 = jnp.float32
    me = lax.axis_index("space")
    tm = lax.axis_index("tm")
    chips = n // 2
    chip = me // 2
    core = me % 2
    mate = chip * 2 + 1 - core
    nvec = v_ref.shape[2]
    sites = v_ref.shape[3]
    own = nvec // n
    half = nvec // 2
    lanes = 2 * nvec
    reach = half // 2
    share = own * reach
    per_half = n // 2
    wide = half + reach
    block_rows = wide * reach
    side = me // per_half
    other_side = 1 - side
    first = (me % per_half) * own
    combos = spin_ref.shape[0]
    count = combos * 3 * own
    low = -(-count // 16) * 16

    def partner(m, back=False):
        if chips & (chips - 1):
            return (chip + chips - m) % chips if back else (chip + m) % chips
        out, bit = 0, 1
        while bit < chips:
            mine, its = chip // bit % 2, m // bit % 2
            out = out + bit * (mine + its - 2 * mine * its)
            bit *= 2
        return out

    barrier = pltpu.get_barrier_semaphore()
    for r in range(1, n):
        pl.semaphore_signal(barrier, inc=1, device_id=(tm, (me + r) % n), device_id_type=MESH)
    for r in range(1, times):
        pl.semaphore_signal(
            barrier, inc=1, device_id=((tm + r) % times, me), device_id_type=MESH
        )

    vec_loads = [
        [
            pltpu.make_async_copy(v_hbm.at[c, a], v_ref.at[c, a], in_sem.at[c * 3 + a])
            for a in range(3)
        ]
        for c in range(2)
    ]
    mat_load = pltpu.make_async_copy(mats_hbm, mats_ref, in_sem.at[6])
    shift_load = pltpu.make_async_copy(shift_hbm, shift_ref, in_sem.at[7])
    for a in range(3):
        vec_loads[0][a].start()
        vec_loads[1][a].start()

    for a in range(3):
        vec_loads[0][a].wait()
        vec_loads[1][a].wait()
        re = v_ref[0, a]
        im = v_ref[1, a]
        re_hi, re_lo = halves(re)
        im_hi, im_lo = halves(im)
        one = pl.ds(a * sites, sites)
        two = pl.ds((3 + a) * sites, sites)
        lead[0:nvec, one] = re_hi
        lead[0:nvec, two] = -im_hi
        lead[nvec:lanes, one] = im_hi
        lead[nvec:lanes, two] = re_hi
        lead[lanes:lanes + nvec, one] = re_lo
        lead[lanes:lanes + nvec, two] = -im_lo
        lead[lanes + nvec:2 * lanes, one] = im_lo
        lead[lanes + nvec:2 * lanes, two] = re_lo
        for c, value in enumerate((re, im)):
            for hf in range(2):
                part = value[hf * half:(hf + 1) * half]
                for b in range(sites // 128):
                    cut = part[:, b * 128:(b + 1) * 128]
                    vv[c, a, b, pl.ds(2 * hf * wide, half, stride=2), :] = cut
                    vv[c, a, b, pl.ds(2 * (hf * wide + half), reach, stride=2), :] = cut[:reach]

    mat_load.start()
    shift_load.start()

    def fill(dest, slot, buf):
        base = (dest // per_half) * wide + (dest % per_half) * own
        for a in range(own):
            at = pl.ds(slot * share + a * reach, reach)
            for cut in range(sites // 128):
                mine = [[vv[c, x, cut, pl.ds(2 * (base + a), 1), :] for x in range(3)] for c in range(2)]
                other = [
                    [vv[c, x, cut, pl.ds(2 * (base + a + 1), reach, stride=2), :] for x in range(3)]
                    for c in range(2)
                ]
                for m in range(3):
                    b, d = (m + 1) % 3, (m + 2) % 3
                    real_part = (
                        mine[0][b] * other[0][d] - mine[1][b] * other[1][d]
                        - (mine[0][d] * other[0][b] - mine[1][d] * other[1][b])
                    )
                    imag_part = (
                        mine[0][b] * other[1][d] + mine[1][b] * other[0][d]
                        - (mine[0][d] * other[1][b] + mine[1][d] * other[0][b])
                    )
                    for q, value in ((m, real_part), (3 + m, imag_part)):
                        hi, lo = halves(value)
                        where = q * sites + cut * 128
                        d_hi[buf, at, where:where + 128] = hi
                        d_lo[buf, at, where:where + 128] = lo

    def pair_copy(s):
        return pltpu.make_async_remote_copy(
            give.at[s], pair_in.at[s], pair_send.at[s], pair_recv.at[s],
            device_id=(tm, mate), device_id_type=MESH,
        )

    def chip_copy(s):
        return pltpu.make_async_remote_copy(
            keep.at[s], chip_in.at[s], chip_send.at[s], chip_recv.at[s],
            device_id=(tm, partner(chips - 1 - s) * 2 + core), device_id_type=MESH,
        )

    def fills(group, buf):
        for slot, (part, s) in enumerate(group):
            fill(partner(chips - 1 - s) * 2 + (1 - core if part == 0 else core), slot, buf)

    def products(group, buf):
        at = pl.ds(0, len(group) * share)
        both = lax.dot_general(d_hi[buf, at, :], lead[...], NT_DIMS, preferred_element_type=f32)
        rest = lax.dot_general(d_lo[buf, at, :], lead[0:lanes], NT_DIMS, preferred_element_type=f32)
        got = both[:, :lanes] + (both[:, lanes:] + rest)
        for slot, (part, s) in enumerate(group):
            (give, keep)[part][s] = got[slot * share:(slot + 1) * share]

    def add_pair(s):
        pair_copy(s).wait_recv()
        keep[s] = keep[s] + pair_in[s]

    outer = chip % 3 == 0
    through = pltpu.make_async_remote_copy(
        keep.at[0], through_in, through_send, through_recv,
        device_id=(tm, partner(1) * 2 + core), device_id_type=MESH,
    )

    def relay(s):
        pair_copy(s).wait_recv()
        keep[s] = keep[s] + pair_in[s]
        chip_copy(s).start()

    def one_chip(s, carry):
        for part in range(2):
            fill(partner(chips - 1 - s) * 2 + (1 - core if part == 0 else core), part, 0)
        both = lax.dot_general(d_hi[0], lead[...], NT_DIMS, preferred_element_type=f32)
        rest = lax.dot_general(d_lo[0], lead[0:lanes], NT_DIMS, preferred_element_type=f32)
        got = both[:, :lanes] + (both[:, lanes:] + rest)
        give[s] = got[:share]
        keep[s] = got[share:]
        pair_copy(s).start()

        @pl.when(s > 0)
        def _():
            relay(s - 1)

        return carry

    if chips == 4:
        groups = (((0, 0),), ((0, 1), (0, 2)), ((1, 0),), ((1, 1), (1, 2)), ((0, 3), (1, 3)))
        fills(groups[0], 0)
        for k, group in enumerate(groups):
            products(group, k % 2)
            if k + 1 < len(groups):
                fills(groups[k + 1], (k + 1) % 2)
            if k == 0:
                pl.semaphore_wait(barrier, n - 1 + times - 1)
            for part, s in group:
                if part == 0:
                    pair_copy(s).start()
            if k == 2:
                add_pair(0)
                pl.when(outer)(through.start)
                pl.when(jnp.logical_not(outer))(chip_copy(0).start)
        add_pair(1)
        pl.when(outer)(chip_copy(1).start)
        relay(2)

        @pl.when(jnp.logical_not(outer))
        def _():
            through.wait_recv()
            keep[1] = keep[1] + through_in[...]
            chip_copy(1).start()

    else:
        pl.semaphore_wait(barrier, n - 1 + times - 1)
        lax.fori_loop(0, chips, one_chip, 0)

    lane = lax.broadcasted_iota(jnp.int32, (half, lanes), 1)
    spot = lane % nvec
    left = spot < half
    real = lane < nvec
    minus_plus = jnp.where(lax.broadcasted_iota(jnp.int32, (nvec, lanes), 1) < nvec, -1.0, 1.0)

    def weave(ref):
        even = ref[pl.ds(0, half, stride=2), :]
        odd = ref[pl.ds(1, half, stride=2), :]
        return (
            jnp.where(real, even, pltpu.roll(odd, nvec, 1)),
            jnp.where(real, pltpu.roll(even, nvec, 1), odd),
        )

    pairs = ((1, 2), (0, 2), (0, 1))
    mat_load.wait()
    shift_load.wait()
    for s in range(combos):
        for q in range(3):
            board[...] = mats_ref[spin_ref[s, q]]
            even, odd = weave(board)
            spin_mats[s, q, pl.ds(0, half, stride=2), :] = even
            spin_mats[s, q, pl.ds(1, half, stride=2), :] = odd
            near = spin_mats[s, q, pl.ds(pl.multiple_of(side * half, half), half), :]
            far = spin_mats[s, q, pl.ds(pl.multiple_of(other_side * half, half), half), :]
            local = jnp.concatenate([near, far], axis=0)
            local_mats[s, q] = local
            parts = halves(local) + halves(minus_plus * pltpu.roll(local, nvec, 1))
            for p in range(3):
                if q in pairs[p]:
                    at = pairs[p].index(q) * lanes
                    for row, top, low_part in ((0, parts[0], parts[2]), (lanes, parts[1], parts[3])):
                        right_hl[s * 3 + p, at:at + nvec, row:row + lanes] = top
                        right_hl[s * 3 + p, at + nvec:at + lanes, row:row + lanes] = low_part
    flat = [(s, q) for s in range(combos) for q in range(3)]
    wide_real = lax.broadcasted_iota(jnp.int32, (nvec, lanes), 1) < nvec
    for m in range(0, len(flat), 2):
        ahead = flat[m + 1] if m + 1 < len(flat) else flat[m]
        t = jnp.transpose(jnp.concatenate([local_mats[flat[m]], local_mats[ahead]], axis=0))
        up, down = t[:nvec], t[nvec:]
        here = jnp.where(wide_real, up, pltpu.roll(down, nvec, 1))
        there = jnp.where(wide_real, pltpu.roll(up, nvec, 1), down)
        for k, value in ((m, here), (m + 1, there)):
            if k < len(flat):
                hi, lo = halves(value)
                left_hl[k * nvec:(k + 1) * nvec, 0:lanes] = hi
                left_hl[k * nvec:(k + 1) * nvec, lanes:2 * lanes] = lo
    for s in range(combos):
        for p in range(3):
            if own % 8 == 0:
                rows = spin_mats[s, p, pl.ds(pl.multiple_of(me * own, own), own), :]
                mid_ref[(s * 3 + p) * own:(s * 3 + p + 1) * own, :] = rows
            else:
                for r in range(own):
                    at = (s * 3 + p) * own + r
                    mid_ref[at:at + 1, :] = spin_mats[s, p, pl.ds(me * own + r, 1), :]

    last = chips - 1
    pair_copy(last).wait_recv()
    total = keep[last] + pair_in[last]
    if chips == 4:
        for s in (1, 2):
            chip_copy(s).wait_recv()
            total = total + chip_in[s]
        own_ref[...] = total * scale

        @pl.when(jnp.logical_not(outer))
        def _():
            chip_copy(0).wait_recv()
            own_ref[...] = (total + chip_in[0]) * scale
    else:
        for s in range(last):
            chip_copy(s).wait_recv()
            total = total + chip_in[s]
        own_ref[...] = total * scale

    def rows_of(d):
        start = (d // per_half) * block_rows + reach * reach + (d % per_half) * share
        return pl.ds(pl.multiple_of(start, reach), share)

    def tm_copy(r):
        return pltpu.make_async_remote_copy(
            own_ref, sink_ref.at[r - 1], tm_send.at[r - 1], tm_recv.at[r - 1],
            device_id=((tm + r) % times, me), device_id_type=MESH,
        )

    def own_copy(r):
        target = mate if r == 0 else partner(r) * 2 + core
        return pltpu.make_async_remote_copy(
            own_ref, full.at[rows_of(me)], own_send.at[r], own_recv.at[r],
            device_id=(tm, target), device_id_type=MESH,
        )

    def forward(r):
        at = rows_of(partner(r, True) * 2 + core)
        return pltpu.make_async_remote_copy(
            full.at[at], full.at[at], fwd_send.at[r - 1], fwd_recv.at[r - 1],
            device_id=(tm, mate), device_id_type=MESH,
        )

    for r in range(1, times):
        tm_copy(r).start()
    for r in range(chips - 1, 0, -1):
        own_copy(r).start()
    own_copy(0).start()
    full[rows_of(me), :] = own_ref[...]

    for r in range(1, times):
        tm_copy(r).wait_recv()
    chosen = sink_ref[jnp.clip(times - 1 - shift_ref[0], 0, times - 2)]
    wide_lane = lax.broadcasted_iota(jnp.int32, (share, lanes), 1)
    wide_left = wide_lane % nvec < half
    swapped = jnp.where(wide_left, pltpu.roll(chosen, lanes - half, 1), pltpu.roll(chosen, half, 1))
    chosen = jnp.where(side == 1, swapped, chosen)
    step_of = lax.broadcasted_iota(jnp.int32, (share, lanes), 0) % reach
    factor = jnp.where(wide_left, 1.0 / 3.0, 1.0) * jnp.where(step_of == reach - 1, 0.5, 1.0)
    chosen = chosen * jnp.where(wide_lane < nvec, factor, -factor)
    placed[...] = jnp.zeros_like(placed)
    for a in range(own):
        if own % 8 == 0:
            start = pl.multiple_of(a * wide + first, 8)
            view = placed.at[pl.ds(start, own + reach), :]
            view[a + 1:a + 1 + reach, :] = chosen[a * reach:(a + 1) * reach]
        else:
            for r in range(reach):
                at = a * wide + first + a + 1 + r
                placed[pl.ds(at, 1), :] = chosen[a * reach + r:a * reach + r + 1]
    around = [
        placed[a * wide:a * wide + half, :] + jnp.concatenate(
            [placed[a * wide + half:(a + 1) * wide, :], jnp.zeros((half - reach, lanes), f32)], axis=0
        )
        for a in range(own)
    ]
    fold = lanes // half
    for g in range(0, own, fold):
        group = (around[g:g + fold] * fold)[:fold]
        t = jnp.transpose(jnp.concatenate(group, axis=0))
        for a in range(g, min(g + fold, own)):
            at = (a % fold) * half
            back = (lanes - at) % lanes

            def to_left(re, im):
                re = pltpu.roll(re, back, 1) if back else re
                im = pltpu.roll(im, (back + nvec) % lanes, 1) if (back + nvec) % lanes else im
                return jnp.where(left, jnp.where(real, re, im), 0.0)

            top = around[a] - to_left(t[:half], t[nvec:nvec + half])
            bottom = -to_left(t[half:nvec], t[nvec + half:])
            value = jnp.concatenate([top, bottom], axis=0)
            hi, lo = halves(value)
            low_hi, low_lo = halves(minus_plus * pltpu.roll(value, nvec, 1))
            at = pl.ds(a * lanes, lanes)
            for start in (0, lanes):
                dense_hh[start:start + nvec, at] = hi
                dense_hh[start + nvec:start + lanes, at] = low_hi
            dense_lo[0:nvec, at] = lo
            dense_lo[nvec:lanes, at] = low_lo

    mats_count = combos * 3
    for a in range(0, own, 2):
        at = pl.ds(a * lanes, 2 * lanes)
        got = dot(left_hl[...], dense_hh[:, at]) + dot(left_hl[:, 0:lanes], dense_lo[:, at])
        for b in range(2):
            inner_ref[pl.ds(a + b, mats_count * nvec, stride=own), :] = got[:, b * lanes:(b + 1) * lanes]
    rows = nvec * own
    for r in range(1, chips):
        own_copy(r).wait_recv()
        forward(r).start()
    def at_row(ref, k, some):
        return jnp.concatenate(
            [ref[(m * half + k) * own:(m * half + k + 1) * own, :] for m in some], axis=0
        )

    def pack(some):
        begin, size = some[0] * own, len(some) * own
        first_lanes = lax.broadcasted_iota(jnp.int32, (size, lanes), 1) < nvec
        for m in range(half // 2):
            even = at_row(same_w, 2 * m, some)
            odd = at_row(same_w, 2 * m + 1, some)
            re = jnp.where(first_lanes, even, pltpu.roll(odd, nvec, 1))
            im = jnp.where(first_lanes, pltpu.roll(even, nvec, 1), odd)
            at = pl.ds(m * lanes, lanes)
            for start, value in ((begin, re), (low + begin, im)):
                hi, lo = halves(value)
                lc_hi[start:start + size, at] = hi
                lc_lo[start:start + size, at] = lo

    parts_of = 2 if combos % 2 == 0 and count // 2 % 16 == 0 else 1
    near_lane = lax.broadcasted_iota(jnp.int32, (rows // 2, lanes), 1) % nvec < half
    for s in range(combos):
        for p in range(3):
            q, r = pairs[p]
            m = s * 3 + p
            at_q = pl.ds((s * 3 + q) * rows, rows)
            at_r = pl.ds((s * 3 + r) * rows, rows)
            left_hi, left_lo = halves(jnp.concatenate([inner_ref[at_r, :], inner_ref[at_q, :]], axis=1))
            both = dot(left_hi, right_hl[m])
            whole = both[:, :lanes] + (both[:, lanes:] + dot(left_lo, right_hl[m, :, 0:lanes]))
            up, down = whole[:rows // 2], whole[rows // 2:]
            at = pl.ds(m * (rows // 2), rows // 2)
            cross_w[at, :] = jnp.where(near_lane, down, up)
            same_w[at, :] = -0.5 * jnp.where(near_lane, up, down)
        if (s + 1) % (combos // parts_of) == 0:
            done = mats_count // parts_of
            pack(range((s + 1) * 3 - done, (s + 1) * 3))

    c_real = lax.broadcasted_iota(jnp.int32, (count, lanes), 1) < nvec
    own_copy(0).wait_recv()
    for r in range(1, chips):
        forward(r).wait_recv()
    for hf in range(2):
        at = hf * block_rows
        full[at:at + reach * reach, :] = full[at + half * reach:at + block_rows, :]

    inner = lax.broadcasted_iota(jnp.int32, (reach, lanes), 0)
    spot64 = lax.broadcasted_iota(jnp.int32, (nvec, lanes), 1) % nvec
    row64 = lax.broadcasted_iota(jnp.int32, (nvec, lanes), 0)
    crossing = (spot64 >= half) == (row64 < half)
    c_sign = jnp.where(c_real, -1.0, 1.0)
    mid = mid_ref[...]
    turned = pltpu.roll(mid, nvec, 1)
    pad = [jnp.zeros((low - count, nvec), jnp.bfloat16)] if low > count else []
    re_hi, re_lo = halves(mid[:, :nvec])
    im_hi, im_lo = halves(turned[:, :nvec])
    mid_hi = jnp.concatenate([re_hi] + pad + [im_hi], axis=0)
    mid_lo = jnp.concatenate([re_lo] + pad + [im_lo], axis=0)
    mid_k = jnp.concatenate([mid_hi, mid_hi, mid_lo], axis=1)
    one = jnp.zeros((count, lanes), f32)
    two = jnp.zeros((count, lanes), f32)
    got_same = None
    for y in range(0, half, 2):
        pair = []
        for k in (y, y + 1):
            parts = []
            for hf in range(2):
                at = hf * block_rows
                before = full[pl.ds(at + reach * k + reach - 1, reach, stride=reach - 1), :]
                behind = full[pl.ds(at + reach * reach + reach * k - 1, reach), :]
                behind = jnp.where(inner == 0, 0.0, -behind)
                slab = jnp.concatenate([before, behind], axis=0)
                shift = (k - reach) % half
                if shift:
                    slab = pltpu.roll(slab, shift, 0)
                slabs[hf * half + k] = slab
                parts.append(slab)
            slab = jnp.concatenate(parts, axis=0)
            hi, lo = halves(slab)
            sl_hl[k * nvec:(k + 1) * nvec, 0:lanes] = hi
            sl_hl[k * nvec:(k + 1) * nvec, lanes:2 * lanes] = lo
            m_hi, m_lo = halves(jnp.where(crossing, slab, 0.0))
            pair.append(jnp.concatenate([m_hi, m_lo, m_hi], axis=0))
        got = dot(mid_k, jnp.concatenate(pair, axis=1))
        for b, k in enumerate((y, y + 1)):
            here = got[:, b * lanes:(b + 1) * lanes]
            value = here[:count] + c_sign * pltpu.roll(here[low:low + count], nvec, 1)
            weight = at_row(cross_w, k, range(mats_count))
            one = one + value * weight
            two = two + value * pltpu.roll(weight, nvec, 1)
        if (y + 2) % (half // 4) == 0:
            at = pl.ds((y + 2 - half // 4) * nvec, half // 4 * nvec)
            both = dot(lc_hi[:, at], sl_hl[at, :])
            both = both[:, :lanes] + (both[:, lanes:] + dot(lc_lo[:, at], sl_hl[at, 0:lanes]))
            got_same = both if got_same is None else got_same + both
    got = got_same
    value = got[:count] + c_sign * pltpu.roll(got[low:low + count], nvec, 1)
    one = one + value * mid
    two = two + value * turned
    one = jnp.where(c_real, one, -one)
    each = 3 * own
    tile_ref[...] = jnp.concatenate(
        [jnp.sum(one[s * each:(s + 1) * each], axis=0, keepdims=True) for s in range(combos)]
        + [jnp.sum(two[s * each:(s + 1) * each], axis=0, keepdims=True) for s in range(combos)],
        axis=0,
    )

    def sum_copy(r):
        return pltpu.make_async_remote_copy(
            tile_ref, box.at[r - 1], sum_send.at[r - 1], sum_recv.at[r - 1],
            device_id=(tm, (me + r) % n), device_id_type=MESH,
        )

    for r in range(1, n):
        sum_copy(r).start()

    for g in range(half // fold):
        t = jnp.transpose(jnp.concatenate(
            [slabs[other_side * half + g * fold + q] for q in range(fold)], axis=0
        ))
        turn[...] = t
        if own % 8 == 0:
            at = pl.multiple_of(side * half + first, own)
            pick[0, g * own:(g + 1) * own, :] = turn[pl.ds(at, own), :]
            pick[1, g * own:(g + 1) * own, :] = turn[pl.ds(at + nvec, own), :]
        else:
            for r in range(own):
                at = side * half + first + r
                pick[0, g * own + r:g * own + r + 1, :] = turn[pl.ds(at, 1), :]
                pick[1, g * own + r:g * own + r + 1, :] = turn[pl.ds(at + nvec, 1), :]
    steps = half // fold
    quarter = lax.broadcasted_iota(jnp.int32, (steps, lanes), 1) // half
    o_left = lax.broadcasted_iota(jnp.int32, (steps, lanes), 1) % nvec < half

    def shifted(x, by):
        by = by % lanes
        return pltpu.roll(x, by, 1) if by else x

    for g in range(0, own, fold):
        group = [slabs[side * half + first + a] for a in range(g, min(g + fold, own))]
        turn[...] = jnp.transpose(jnp.concatenate((group * fold)[:fold], axis=0))
        at = pl.multiple_of(other_side * half, half)
        re = turn[pl.ds(at, half), :]
        im = turn[pl.ds(at + nvec, half), :]
        turn[0:half, :] = re
        turn[half:2 * half, :] = im
        for a in range(g, min(g + fold, own)):
            for q in range(fold):
                x_re = turn[pl.ds(q, steps, stride=fold), :]
                x_im = turn[pl.ds(half + q, steps, stride=fold), :]
                c_re = pick[0, pl.ds(a, steps, stride=own), :]
                c_im = pick[1, pl.ds(a, steps, stride=own), :]
                back = (a % fold) * half
                value = jnp.where(
                    quarter < 2,
                    jnp.where(quarter == 0, -shifted(x_re, -back), shifted(c_re, half - q * half)),
                    jnp.where(quarter == 2, -shifted(x_im, nvec - back), shifted(c_im, nvec + half - q * half)),
                )
                flipped = jnp.where(o_left, pltpu.roll(value, lanes - half, 1), pltpu.roll(value, half, 1))
                value = jnp.where(side == 1, flipped, value)
                placed[pl.ds(q, steps, stride=fold), :] = value
            board[pl.ds(pl.multiple_of(side * half, half), half), :] = slabs[side * half + first + a]
            board[pl.ds(pl.multiple_of(other_side * half, half), half), :] = placed[0:half, :]
            even, odd = weave(board)
            out_ref[a, pl.ds(0, half, stride=2), :] = even
            out_ref[a, pl.ds(1, half, stride=2), :] = odd

    for s in range(chips):
        pair_copy(s).wait_send()
    if chips == 4:
        pl.when(outer)(through.wait_send)
        pl.when(jnp.logical_not(outer))(chip_copy(0).wait_send)
        chip_copy(1).wait_send()
        chip_copy(2).wait_send()
    else:
        for s in range(chips - 1):
            chip_copy(s).wait_send()
    for r in range(1, times):
        tm_copy(r).wait_send()
    own_copy(0).wait_send()
    for r in range(1, chips):
        own_copy(r).wait_send()
        forward(r).wait_send()
    answer = tile_ref[...]
    for r in range(1, n):
        sum_copy(r).wait_recv()
        answer = answer + box[r - 1]
    total = jnp.sum(jnp.transpose(answer), axis=0, keepdims=True) * corr_scale
    corr_ref[...] = jnp.concatenate([total[:, :combos], total[:, combos:]], axis=0)
    for r in range(1, n):
        sum_copy(r).wait_send()


def shards(vectors, perambulators, shift_steps, spin_choice):
    vec = vectors[0]
    _, _, nvec, sites = vec.shape
    spin_pairs = perambulators.shape[1]
    combos = spin_choice.shape[0]
    n = lax.axis_size("space")
    times = lax.axis_size("tm")
    own, half, lanes = nvec // n, nvec // 2, 2 * nvec
    reach = half // 2
    wide = half + reach
    share = own * reach
    chips = n // 2
    count = combos * 3 * own
    low = -(-count // 16) * 16
    scale = 1.0 / math.sqrt(24.0 * sites * n)
    corr_scale = 0.25 / (nvec * math.sqrt(nvec))
    mats = perambulators[0].reshape(spin_pairs, 2, half, lanes)
    mats = jnp.transpose(mats, (0, 2, 1, 3)).reshape(spin_pairs, nvec, lanes)
    tile = (share, lanes)
    f32, bf16 = jnp.float32, jnp.bfloat16
    dma = pltpu.SemaphoreType.DMA
    smem = pl.BlockSpec(memory_space=pltpu.SMEM)
    anywhere = pl.BlockSpec(memory_space=pl.ANY)
    out, correlator = pl.pallas_call(
        functools.partial(elementals_kernel, n, times, scale, corr_scale),
        out_shape=(
            pltpu.VMEM((own, nvec, lanes), f32),
            pltpu.VMEM((2, combos), f32),
        ),
        in_specs=[anywhere, anywhere, anywhere, smem],
        out_specs=(VM, VM),
        scratch_shapes=[
            pltpu.VMEM(vec.shape, f32),
            pltpu.VMEM(mats.shape, f32),
            pltpu.SMEM(shift_steps.shape, jnp.int32),
            dma((8,)),
            pltpu.VMEM((2, 3, sites // 128, 4 * wide, 128), f32),
            pltpu.VMEM((4 * nvec, 6 * sites), bf16),
            pltpu.VMEM((2, 2 * share, 6 * sites), bf16),
            pltpu.VMEM((2, 2 * share, 6 * sites), bf16),
            pltpu.VMEM((chips,) + tile, f32),
            pltpu.VMEM((chips,) + tile, f32),
            pltpu.VMEM((chips,) + tile, f32),
            pltpu.VMEM((chips - 1,) + tile, f32),
            pltpu.VMEM(tile, f32),
            pltpu.VMEM((2 * wide * reach, lanes), f32),
            pltpu.VMEM((times - 1,) + tile, f32),
            pltpu.VMEM((nvec, lanes), f32),
            pltpu.VMEM((combos, 3, nvec, lanes), f32),
            pltpu.VMEM((combos, 3, nvec, lanes), f32),
            pltpu.VMEM((combos * 3, 2 * lanes, 2 * lanes), bf16),
            pltpu.VMEM((combos * 3 * nvec, 2 * lanes), bf16),
            pltpu.VMEM((max(own, 2) * wide, lanes), f32),
            pltpu.VMEM((2 * lanes, own * lanes), bf16),
            pltpu.VMEM((lanes, own * lanes), bf16),
            pltpu.VMEM((combos * 3 * nvec * own, lanes), f32),
            pltpu.VMEM((count * half, lanes), f32),
            pltpu.VMEM((count * half, lanes), f32),
            pltpu.VMEM((2 * low, half * nvec), bf16),
            pltpu.VMEM((2 * low, half * nvec), bf16),
            pltpu.VMEM((count, lanes), f32),
            pltpu.VMEM((nvec, half, lanes), f32),
            pltpu.VMEM((half * nvec, 2 * lanes), bf16),
            pltpu.VMEM((lanes, lanes), f32),
            pltpu.VMEM((2, own * (nvec // 8), lanes), f32),
            pltpu.VMEM((2 * combos, lanes), f32),
            pltpu.VMEM((n - 1, 2 * combos, lanes), f32),
            dma((chips,)), dma((chips,)),
            dma((chips - 1,)), dma((chips - 1,)),
            dma((chips,)), dma((chips,)),
            dma((chips - 1,)), dma((chips - 1,)),
            dma((times - 1,)), dma((times - 1,)),
            dma((n - 1,)), dma((n - 1,)),
            pltpu.VMEM(tile, f32), dma, dma,
        ],
        compiler_params=pltpu.CompilerParams(
            collective_id=0, has_side_effects=True, vmem_limit_bytes=60 * 1024 * 1024
        ),
        name="elementals",
    )(vec, mats, shift_steps, spin_choice)
    out = jnp.transpose(out.reshape(own, half, 2, lanes), (0, 2, 1, 3))
    return (out.reshape(1, own, 2, nvec * nvec), jnp.transpose(correlator)[None])


def solution(mesh):
    placed = (P("tm", None, None, None, "space"), P("tm", None, None, None), P("tm"), P())
    return jax.shard_map(
        shards,
        mesh=mesh,
        in_specs=placed,
        out_specs=(P("tm", "space", None, None), P("tm", None, None)),
        check_vma=False,
    )
```
